256 devices in a mesh: dp: 4 (over y), pipe: 2 (over core), gz: 8 (over z), gy: 4 (over x).
Axes of the slice: x: 4, y: 4, z: 8, core: 2. Of those that a mesh axis runs over, the one named last changes fastest.
Arguments:
- volumes: bfloat16 [8, 32, 16, 32, 128], P('dp', None, 'gz', 'gy'), may hold values from -6 to 6
- conv_one: bfloat16 [32, 4, 3, 3, 3], replicated, may hold values from -0.625 to 0.625
- conv_two: bfloat16 [64, 32, 3, 3, 3], replicated, may hold values from -0.21875 to 0.21875
- cotangent: bfloat16 [8, 64, 8, 16, 64], P('dp', None, 'gz', 'gy'), may hold values from -24 to 24
Outputs:
- boundary_acts: bfloat16 [8, 32, 16, 32, 128], P('dp', None, 'gz', 'gy')
- boundary_grads: bfloat16 [8, 32, 16, 32, 128], P('dp', None, 'gz', 'gy')
- grad_conv_one: float32 [32, 4, 3, 3, 3], replicated
- grad_conv_two: float32 [64, 32, 3, 3, 3], replicated
The draws below stay inside these ranges and needn't reach their ends.
All inputs are finite; a program needn't handle non-finite values.
Results may differ from the reference program's by a relative error of at most 0.0085.
Values may be sent and summed in bfloat16 or wider, within the bound.
A program may use at most 128 MiB of HBM per device.

```python
import math
import jax
import jax.numpy as jnp
from jax import lax

C_IN = 4
C_ONE = 32
C_TWO = 64
CX = 128
BATCH = 8
NZ = 16
NY = 32


def shard_levels(stream_key, dims, cuts, least, largest):
    level, own = 1.0, jax.random.fold_in(stream_key, 6)
    for axis_at, shards_of in cuts:
        draws = jnp.exp(jax.random.uniform(jax.random.fold_in(own, axis_at), (shards_of,), jnp.float32, least / len(cuts), largest / len(cuts)))
        level = level * jnp.repeat(draws, dims[axis_at] // shards_of).reshape([-1 if axis == axis_at else 1 for axis in range(len(dims))])
    return level


def gaussian(own_key, extent, width, most, shards=(), held_as=jnp.bfloat16):
    values = jax.random.normal(own_key, extent, jnp.float32) * width
    if len(shards) > 0:
        values = shard_levels(own_key, extent, shards, -0.22, 0.18) * values
    return jnp.clip(values, min=-most, max=most).astype(held_as)


def setup_inputs(seed: int = 0) -> dict:
    streams_of = jax.random.split(jax.random.key(seed), 5)
    volumes = gaussian(streams_of[0], (BATCH, 8 * C_IN, NZ, NY, CX), 1.0, 6.0, ((0, 4), (2, 8), (3, 4)))
    conv_one = gaussian(streams_of[1], (C_ONE, C_IN, 3, 3, 3), (C_IN * 27) ** -0.5, 0.625)
    conv_two = gaussian(streams_of[2], (C_TWO, C_ONE, 3, 3, 3), (C_ONE * 27) ** -0.5, 0.21875)
    cotangent = gaussian(streams_of[3], (BATCH, C_TWO, NZ // 2, NY // 2, CX // 2), 4.0, 24.0, ((0, 4), (2, 8), (3, 4)))
    return dict(volumes=volumes, conv_one=conv_one, conv_two=conv_two, cotangent=cotangent)


LEAK_SLOPE = 0.3
LOG_TWO = math.log(2.0)
LAYOUT = ('NCDHW', 'OIDHW', 'NCDHW')

def activate(pre_act):
    return LEAK_SLOPE * pre_act + (1.0 - LEAK_SLOPE) * (jax.nn.softplus(pre_act) - LOG_TWO)

def derivative(pre_act):
    return LEAK_SLOPE + (1.0 - LEAK_SLOPE) * jax.nn.sigmoid(pre_act)

def unfold(coarse):
    span_z, span_y, span_x = coarse.shape[1:]
    pieces = coarse.reshape(2, 2, 2, -1, span_z, span_y, span_x)
    ordered = pieces.transpose(3, 4, 0, 5, 1, 6, 2)
    return ordered.reshape(-1, 2 * span_z, 2 * span_y, 2 * span_x)

def average_blocks(grid_in):
    chan_count, span_z, span_y, span_x = grid_in.shape
    grouped = grid_in.reshape(chan_count, span_z // 2, 2, span_y // 2, 2, span_x // 2, 2)
    return lax.optimization_barrier(jnp.mean(grouped, axis=(2, 4, 6)))

def spread_blocks(grid_in):
    chan_count, span_z, span_y, span_x = grid_in.shape
    copied = jnp.broadcast_to(grid_in[:, :, None, :, None, :, None], (chan_count, span_z, 2, span_y, 2, span_x, 2))
    return copied.reshape(chan_count, 2 * span_z, 2 * span_y, 2 * span_x) / 8.0

def convolve(grid_in, kernel):
    result = lax.conv_general_dilated(grid_in[None], kernel, (1, 1, 1), ((1, 1), (1, 1), (1, 1)), dimension_numbers=LAYOUT, preferred_element_type=jnp.float32)
    return result[0]

def kernel_grad(padded, grad_out):
    out_count = grad_out.shape[0]
    in_count = padded.shape[0]
    span_z, span_y, span_x = grad_out.shape[1:]
    flat_out = grad_out.reshape(out_count, -1)
    products = []
    for off_z in range(3):
        for off_y in range(3):
            for off_x in range(3):
                shifted = padded[:, off_z:off_z + span_z, off_y:off_y + span_y, off_x:off_x + span_x].reshape(in_count, -1)
                products.append(jnp.dot(flat_out, shifted.T, preferred_element_type=jnp.float32))
    return jnp.stack(products, axis=-1).reshape(out_count, in_count, 3, 3, 3)

def reference(volumes, conv_one, conv_two, cotangent):
    flipped = jnp.flip(conv_two, axis=(2, 3, 4)).transpose(1, 0, 2, 3, 4)
    pad_three = ((0, 0), (1, 1), (1, 1), (1, 1))

    def per_volume(totals, sample):
        volume, cot_part = sample
        fine_grid = unfold(volume)
        first_pre = convolve(fine_grid, conv_one)
        pooled = average_blocks(activate(first_pre)).astype(jnp.bfloat16)
        second_pre = convolve(pooled, conv_two)
        second_grad = (derivative(second_pre) * spread_blocks(cot_part.astype(jnp.float32))).astype(jnp.bfloat16)
        back_grad = convolve(second_grad, flipped).astype(jnp.bfloat16)
        first_grad = (derivative(first_pre) * spread_blocks(back_grad.astype(jnp.float32))).astype(jnp.bfloat16)
        grad_one = totals[0] + kernel_grad(jnp.pad(fine_grid, pad_three), first_grad)
        grad_two = totals[1] + kernel_grad(jnp.pad(pooled, pad_three), second_grad)
        return ((grad_one, grad_two), (pooled, back_grad))
    start = (jnp.zeros(conv_one.shape, jnp.float32), jnp.zeros(conv_two.shape, jnp.float32))
    totals, stacked = lax.scan(per_volume, start, (volumes, cotangent))
    return (stacked[0], stacked[1], totals[0] / BATCH, totals[1] / BATCH)
```

```python
import functools
import math

import jax
import jax.numpy as jnp
from jax import lax
from jax.experimental import pallas as pl
from jax.experimental.pallas import tpu as pltpu
from jax.sharding import PartitionSpec as P

LEAK = 0.3
REST = 1.0 - LEAK
LOG_TWO = math.log(2.0)
MESH = pl.DeviceIdType.MESH
F32 = jnp.float32
BF16 = jnp.bfloat16
LANES = 128
DIRS = tuple((dz, dy) for dz in (-1, 0, 1) for dy in (-1, 0, 1) if (dz, dy) != (0, 0))


def mm(a, b):
    return lax.dot_general(a, b, (((1,), (0,)), ((), ())), preferred_element_type=F32)


def mm_nt(a, b):
    return lax.dot_general(a, b, (((1,), (1,)), ((), ())), preferred_element_type=F32)


def eye(n, m):
    return (
        lax.broadcasted_iota(jnp.int32, (n, m), 0) == lax.broadcasted_iota(jnp.int32, (n, m), 1)
    ).astype(BF16)


def to_right(v):
    lane = lax.broadcasted_iota(jnp.int32, v.shape, 1)
    return jnp.where(lane == 0, 0.0, pltpu.roll(v, 1, axis=1))


def to_left(v):
    lane = lax.broadcasted_iota(jnp.int32, v.shape, 1)
    return jnp.where(lane == LANES - 1, 0.0, pltpu.roll(v, LANES - 1, axis=1))


def slope_of(v):
    return LEAK + REST / (1.0 + jnp.exp(-v))


def act_and_slope(v):
    e = jnp.exp(-jnp.abs(v))
    r = 1.0 / (1.0 + e)
    act = LEAK * v + REST * (jnp.maximum(v, 0.0) + jnp.log(1.0 + e) - LOG_TWO)
    return act, LEAK + REST * jnp.where(v >= 0.0, r, e * r)


def part(d, n):
    if d == 0:
        return pl.ds(1, n), pl.ds(1, n)
    if d == 1:
        return pl.ds(n, 1), pl.ds(0, 1)
    return pl.ds(1, 1), pl.ds(n + 1, 1)


def step_kernel(
    dims,
    vol, one_ref, two_ref, cot_ref,
    acts_out, grads_out, one_out, two_out,
    raw, rawf, fine, pool, grad2, slope1, shifted, cots, sel, w1, w2, wb,
    sum1, sum2, flat1, flat2, half1, half2,
    ga, ra, sb, rb, sc, rc, fd,
    qa, qra, qs, qrb, qsc, qrc, qf,
    local_sem, out_ssem, out_rsem,
    h_ssem, h_rsem,
    pair_ssem, pair_rsem, line_ssem, line_rsem, plane_ssem, plane_rsem,
):
    nd, nz, ny, sz, sy, batch = dims
    rows = sz * sy
    core = lax.axis_index("pipe")
    iz, iy, idp = lax.axis_index("gz"), lax.axis_index("gy"), lax.axis_index("dp")
    other = 1 - core
    plane = nd * ny
    me_plane = idp * ny + iy

    def on_line(off):
        return lax.rem(iz + off, nz)

    def on_plane(off):
        q = lax.rem(me_plane + off, plane)
        return q, {"dp": q // ny, "gy": lax.rem(q, ny)}

    def exists(dz, dy):
        ok = jnp.bool_(True)
        if dz == 1:
            ok = jnp.logical_and(ok, iz < nz - 1)
        if dz == -1:
            ok = jnp.logical_and(ok, iz > 0)
        if dy == 1:
            ok = jnp.logical_and(ok, iy < ny - 1)
        if dy == -1:
            ok = jnp.logical_and(ok, iy > 0)
        return ok

    def neighbour(dz, dy):
        return {"gz": lax.rem(iz + dz + nz, nz), "gy": lax.rem(iy + dy + ny, ny)}

    def halo_copy(k, ref, d):
        dz, dy = DIRS[d]
        (fz, tz), (fy, ty) = part(dz, ref.shape[0] - 2), part(dy, ref.shape[1] - 2)
        return pltpu.make_async_remote_copy(
            src_ref=ref.at[fz, fy],
            dst_ref=ref.at[tz, ty],
            send_sem=h_ssem.at[k, d],
            recv_sem=h_rsem.at[k, d],
            device_id=neighbour(dz, dy),
            device_id_type=MESH,
        )

    def halo_clear(ref):
        for dz, dy in DIRS:
            _, tz = part(dz, ref.shape[0] - 2)
            _, ty = part(dy, ref.shape[1] - 2)

            @pl.when(jnp.logical_not(exists(-dz, -dy)))
            def _():
                view = ref.at[tz, ty]
                view[...] = jnp.zeros(view.shape, view.dtype)

    def halo_send(k, ref):
        for d, (dz, dy) in enumerate(DIRS):

            @pl.when(exists(dz, dy))
            def _():
                halo_copy(k, ref, d).start()

    def halo_arrive(k, ref):
        for d, (dz, dy) in enumerate(DIRS):

            @pl.when(exists(-dz, -dy))
            def _():
                halo_copy(k, ref, d).wait_recv()

    def halo_sent(k, ref):
        for d, (dz, dy) in enumerate(DIRS):

            @pl.when(exists(dz, dy))
            def _():
                halo_copy(k, ref, d).wait_send()

    def to_pair(k, src, dst):
        return pltpu.make_async_remote_copy(
            src_ref=src, dst_ref=dst, send_sem=pair_ssem.at[k], recv_sem=pair_rsem.at[k],
            device_id={"pipe": other}, device_id_type=MESH,
        )

    def to_line(k, off, src, dst):
        return pltpu.make_async_remote_copy(
            src_ref=src, dst_ref=dst, send_sem=line_ssem.at[k, off - 1], recv_sem=line_rsem.at[k, off - 1],
            device_id={"gz": on_line(off)}, device_id_type=MESH,
        )

    def to_plane(k, off, src, dst):
        return pltpu.make_async_remote_copy(
            src_ref=src, dst_ref=dst, send_sem=plane_ssem.at[k, off - 1], recv_sem=plane_rsem.at[k, off - 1],
            device_id=on_plane(off)[1], device_id_type=MESH,
        )

    fetch = pltpu.make_async_copy(vol.at[core], raw, local_sem.at[0])
    fetch.start()
    barrier = pltpu.get_barrier_semaphore()
    pl.semaphore_signal(barrier, inc=1, device_id={"pipe": other}, device_id_type=MESH)
    count = jnp.int32(1 + (nz - 1) + (plane - 1))
    for dz, dy in DIRS:
        if dz != 0 and dy != 0:

            @pl.when(exists(dz, dy))
            def _():
                pl.semaphore_signal(barrier, inc=1, device_id=neighbour(dz, dy), device_id_type=MESH)

            count = count + exists(dz, dy).astype(jnp.int32)
    for off in range(1, plane):
        pl.semaphore_signal(barrier, inc=1, device_id=on_plane(off)[1], device_id_type=MESH)
    for off in range(1, nz):
        pl.semaphore_signal(barrier, inc=1, device_id={"gz": on_line(off)}, device_id_type=MESH)

    halo_clear(fine)
    halo_clear(pool)
    halo_clear(grad2)

    fetch.wait()
    rawf[...] = raw[...].astype(F32)

    def spread_row(z, y):
        t = rawf[pl.ds(z * sy + y, 32, stride=rows), :]
        sub = lax.broadcasted_iota(jnp.int32, t.shape, 0)
        odd = (sub & 4) != 0
        low = jnp.where(odd, to_right(t), t)
        high = jnp.where(odd, t, to_left(t))
        for a in range(2):
            for b in range(2):
                j = 8 * (2 * a + b)
                both = jnp.concatenate([low[j : j + 8], high[j : j + 8]], axis=0)
                fine[2 * z + a + 1, 2 * y + b + 1] = both.astype(BF16)

    def loop_rows(body):
        def outer(z, _):
            def inner(y, __):
                body(z, y)
                return 0

            lax.fori_loop(0, sy, inner, 0)
            return 0

        lax.fori_loop(0, sz, outer, 0)

    def loop_pairs(z, body):
        def inner(p, _):
            body(z, p)
            return 0

        lax.fori_loop(0, sy // 2, inner, 0)

    loop_rows(spread_row)
    pl.semaphore_wait(barrier, count)
    halo_send(0, fine)

    row = lax.broadcasted_iota(jnp.int32, (128, 256), 0)
    lane = lax.broadcasted_iota(jnp.int32, (128, 256), 1)
    tap = row >> 2
    by3 = (tap * 11) >> 5
    by9 = (by3 * 11) >> 5
    tx, ty, tz = tap - 3 * by3, by3 - 3 * by9, by9
    for d in range(27):
        qa[0, 4 * d : 4 * d + 4, 0:32] = one_ref[d].astype(F32)
    qa[0, 108:128, 0:32] = jnp.zeros((20, 32), F32)
    one_t = mm_nt(eye(32, 32), qa[0, :, 0:32].astype(BF16)).astype(BF16)
    for s in range(8):
        a, b, c = s >> 2, (s >> 1) & 1, s & 1
        fx = tx + c
        slot = fx + 1 - 2 * (fx & 1)
        target = (tz + a) * 64 + (ty + b) * 16 + slot * 4 + (row & 3)
        hit = jnp.logical_and(lane == target, row < 108)
        sel[s] = jnp.where(hit, 1.0, 0.0).astype(BF16)
        w1[32 * s : 32 * s + 32, :] = mm(one_t, sel[s]).astype(BF16)
    for dx in range(3):
        taps = jnp.concatenate([two_ref[3 * j + dx] for j in range(9)], axis=0)
        w2[64 * dx : 64 * dx + 64, :] = mm_nt(eye(64, 64), taps).astype(BF16)
    for ex in range(3):
        blocks = [two_ref[3 * (8 - j) + 2 - ex].astype(F32) for j in range(9)]
        for j in range(0, 8, 2):
            pair = jnp.concatenate([blocks[j], blocks[j + 1]], axis=1)
            wb[32 * ex : 32 * ex + 32, 64 * j : 64 * j + 128] = pair.astype(BF16)
        wb[32 * ex : 32 * ex + 32, 512:576] = blocks[8].astype(BF16)
    double = (
        (lax.broadcasted_iota(jnp.int32, (64, LANES), 1) >> 1)
        == lax.broadcasted_iota(jnp.int32, (64, LANES), 0)
    ).astype(BF16)
    for y in range(sy // 2):
        cots[y] = mm(cot_ref[core, y], double) * 0.125

    def windows(z, p):
        return jnp.concatenate(
            [fine[pl.ds(2 * z, 4), pl.ds(4 * p + 2 * j, 4)].reshape(256, LANES) for j in range(2)], axis=1
        )

    def first_pair(z, p):
        pre = mm(w1[...], windows(z, p))
        for j in range(2):
            y = 2 * p + j
            total = jnp.zeros((32, LANES), F32)
            for s in range(8):
                act, slope = act_and_slope(pre[32 * s : 32 * s + 32, LANES * j : LANES * j + LANES])
                total = total + act
                slope1[z, y, 32 * s : 32 * s + 32, :] = slope
            mean = total * 0.125
            pool[z + 1, y + 1] = mean.astype(BF16)
            flat1[pl.ds(z * sy + y, 32, stride=rows), :] = mean

    halo_arrive(0, fine)
    for z in range(sz):
        loop_pairs(z, first_pair)
    halo_send(1, pool)
    half1[...] = flat1[...].astype(BF16)

    def out_copies(k, half, out):
        here = pltpu.make_async_copy(half, out.at[core], local_sem.at[1 + k])
        there = pltpu.make_async_remote_copy(
            src_ref=half, dst_ref=out.at[core], send_sem=out_ssem.at[k], recv_sem=out_rsem.at[k],
            device_id={"pipe": other}, device_id_type=MESH,
        )
        return here, there

    for copy in out_copies(0, half1, acts_out):
        copy.start()

    def second_pair(z, p):
        cells = jnp.concatenate(
            [pool[pl.ds(z, 3), pl.ds(2 * p + j, 3)].reshape(288, LANES) for j in range(2)], axis=1
        )
        prod = mm(w2[...], cells)
        for j in range(2):
            mine = prod[:, LANES * j : LANES * j + LANES]
            pre = to_right(mine[0:64]) + mine[64:128] + to_left(mine[128:192])
            g = (slope_of(pre) * cots[p]).astype(BF16)
            grad2[z + 1, 2 * p + j + 1] = g
            wide = g.astype(F32)
            right = to_right(wide).astype(BF16)
            cols = slice(LANES * j, LANES * j + LANES)
            shifted[z, p, 0:64, cols] = to_left(wide).astype(BF16)
            shifted[z, p, 64:128, cols] = g
            shifted[z, p, 128:192, cols] = right
            shifted[z, p, 192:256, cols] = right

    halo_arrive(1, pool)
    for z in range(sz):
        loop_pairs(z, second_pair)
    halo_send(2, grad2)

    sum2[...] = jnp.zeros(sum2.shape, F32)

    def second_terms(z, p):
        cells = jnp.concatenate(
            [pool[pl.ds(z, 3), pl.ds(2 * p + j, 3)].reshape(288, LANES) for j in range(2)], axis=1
        )
        sum2[...] += mm_nt(cells, shifted[z, p])

    for z in range(sz):
        loop_pairs(z, second_terms)
    for r in range(9):
        ga[r // 8, r % 8] = sum2[32 * r : 32 * r + 32, 0:128]
    keep = lax.broadcasted_iota(jnp.int32, (16, LANES), 1) < 64
    for r in range(9):
        lo, hi = sum2[16 * r : 16 * r + 16, 128:256], sum2[144 + 16 * r : 160 + 16 * r, 128:256]
        at = 288 + 16 * r
        ga[at // 256, at % 256 // 32, at % 32 : at % 32 + 16] = jnp.where(keep, lo, hi)
    ga[1, 5, 16:32] = jnp.zeros((16, LANES), F32)
    ga[1, 6] = jnp.zeros((32, LANES), F32)
    ga[1, 7] = jnp.zeros((32, LANES), F32)
    to_pair(0, ga.at[other], ra).start()

    sum1[...] = jnp.zeros(sum1.shape, F32)

    def back_pair(z, p):
        cells = jnp.concatenate(
            [grad2[pl.ds(z, 3), pl.ds(2 * p + j, 3)].reshape(576, LANES) for j in range(2)], axis=1
        )
        prod = mm(wb[...], cells)
        grads = []
        for j in range(2):
            y = 2 * p + j
            mine = prod[:, LANES * j : LANES * j + LANES]
            back = to_right(mine[0:32]) + mine[32:64] + to_left(mine[64:96])
            back = back.astype(BF16).astype(F32)
            flat2[pl.ds(z * sy + y, 32, stride=rows), :] = back
            eighth = back * 0.125
            grads.append(
                jnp.concatenate(
                    [(slope1[z, y, 32 * s : 32 * s + 32, :] * eighth).astype(BF16) for s in range(8)], axis=0
                )
            )
        sum1[...] += mm_nt(jnp.concatenate(grads, axis=1), windows(z, p))

    line = range(1, nz)
    flat = range(1, plane)

    halo_arrive(2, grad2)
    loop_pairs(0, back_pair)
    to_pair(0, ga.at[other], ra).wait_recv()
    for j in range(8):
        sb[j] = ga[core, j] + ra[j]
    for off in line:
        to_line(0, off, sb.at[on_line(off)], rb.at[off - 1]).start()
    for z in range(1, sz):
        loop_pairs(z, back_pair)

    folded = jnp.zeros((32, LANES), F32)
    for s in range(8):
        mine = sum1[32 * s : 32 * s + 32, :]
        high = mine.astype(BF16)
        low = (mine - high.astype(F32)).astype(BF16)
        folded = folded + mm_nt(high, sel[s]) + mm_nt(low, sel[s])
    qs[...] = folded
    to_pair(1, qs, qra).start()
    half2[...] = flat2[...].astype(BF16)
    for copy in out_copies(1, half2, grads_out):
        copy.start()

    for off in line:
        to_line(0, off, sb.at[on_line(off)], rb.at[off - 1]).wait_recv()
    total = sb[iz]
    for off in line:
        total = total + rb[off - 1]
    sc[...] = total
    rc[me_plane] = total
    for off in flat:
        to_plane(0, off, sc, rc.at[me_plane]).start()

    to_pair(1, qs, qra).wait_recv()
    both = qs[...] + qra[...]
    mine = jnp.where(core == 0, both[0:16], both[16:32])
    qsc[0] = mine
    qrb[iz] = mine
    for off in line:
        to_line(1, off, qsc.at[0], qrb.at[iz]).start()

    for off in flat:
        to_plane(0, off, sc, rc.at[me_plane]).wait_recv()
    total = rc[0]
    for q in range(1, plane):
        total = total + rc[q]
    fd[core, iz] = total * (1.0 / batch)
    for off in line:
        to_line(2, off, fd.at[core, iz], fd.at[core, iz]).start()

    for off in line:
        to_line(1, off, qsc.at[0], qrb.at[iz]).wait_recv()
    total = qrb[0]
    for q in range(1, nz):
        total = total + qrb[q]
    qsc[1] = total
    qrc[me_plane] = total
    for off in flat:
        to_plane(1, off, qsc.at[1], qrc.at[me_plane]).start()

    for off in line:
        to_line(2, off, fd.at[core, iz], fd.at[core, iz]).wait_recv()
    to_pair(2, fd.at[core], fd.at[core]).start()

    for off in flat:
        to_plane(1, off, qsc.at[1], qrc.at[me_plane]).wait_recv()
    total = qrc[0]
    for q in range(1, plane):
        total = total + qrc[q]
    qf[core] = total * (1.0 / batch)
    to_pair(3, qf.at[core], qf.at[core]).start()

    to_pair(2, fd.at[core], fd.at[core]).wait_recv()
    for j in range(9):
        block = fd[j // 8, j % 8]
        two_out[3 * j] = block[:, 0:64]
        two_out[3 * j + 1] = pltpu.roll(block, 64, axis=1)[:, 0:64]
    for r in range(9):
        at = 288 + 16 * r
        block = fd[at // 256, at % 256 // 32, at % 32 : at % 32 + 16]
        for first, values in ((16 * r, block), (144 + 16 * r, pltpu.roll(block, 64, axis=1))):
            two_out[3 * (first // 32) + 2, first % 32 : first % 32 + 16, :] = values[:, 0:64]
    to_pair(3, qf.at[core], qf.at[core]).wait_recv()
    turned = jnp.transpose(jnp.concatenate([qf[0], qf[1]], axis=0))
    for d in range(27):
        one_out[d] = turned[4 * d : 4 * d + 4, :]

    for k, ref in enumerate((fine, pool, grad2)):
        halo_sent(k, ref)
    to_pair(0, ga.at[other], ra).wait_send()
    to_pair(1, qs, qra).wait_send()
    to_pair(2, fd.at[core], fd.at[core]).wait_send()
    to_pair(3, qf.at[core], qf.at[core]).wait_send()
    for off in line:
        to_line(0, off, sb.at[on_line(off)], rb.at[off - 1]).wait_send()
        to_line(1, off, qsc.at[0], qrb.at[iz]).wait_send()
        to_line(2, off, fd.at[core, iz], fd.at[core, iz]).wait_send()
    for off in flat:
        to_plane(0, off, sc, rc.at[me_plane]).wait_send()
        to_plane(1, off, qsc.at[1], qrc.at[me_plane]).wait_send()
    for k, (half, out) in enumerate(((half1, acts_out), (half2, grads_out))):
        here, there = out_copies(k, half, out)
        here.wait()
        there.wait()


def solution(mesh):
    nd, nz, ny = mesh.shape["dp"], mesh.shape["gz"], mesh.shape["gy"]
    plane = nd * ny

    def per_device(volumes, conv_one, conv_two, cotangent):
        micro, feats, sz, sy, sx = volumes.shape
        rows = sz * sy
        dims = (nd, nz, ny, sz, sy, micro * nd)
        vol = volumes.reshape(micro, feats * rows, sx)
        one = conv_one.transpose(2, 3, 4, 1, 0).reshape(27, 4, 32)
        two = conv_two.transpose(2, 3, 4, 1, 0).reshape(27, 32, 64)
        cot = cotangent[:, :, 0].transpose(0, 2, 1, 3)
        whole = pl.BlockSpec(memory_space=pltpu.VMEM)
        away = pl.BlockSpec(memory_space=pl.ANY)
        vmem = pltpu.VMEM
        dma = pltpu.SemaphoreType.DMA
        acts, grads, g_one, g_two = pl.pallas_call(
            functools.partial(step_kernel, dims),
            out_shape=(
                jax.ShapeDtypeStruct(vol.shape, BF16),
                jax.ShapeDtypeStruct(vol.shape, BF16),
                jax.ShapeDtypeStruct((27, 4, 32), F32),
                jax.ShapeDtypeStruct((27, 32, 64), F32),
            ),
            in_specs=[away, whole, whole, whole],
            out_specs=(away, away, whole, whole),
            scratch_shapes=[
                vmem((feats * rows, sx), BF16),
                vmem((feats * rows, sx), F32),
                vmem((2 * sz + 2, 2 * sy + 2, 16, sx), BF16),
                vmem((sz + 2, sy + 2, 32, sx), BF16),
                vmem((sz + 2, sy + 2, 64, sx), BF16),
                vmem((sz, sy, 256, sx), F32),
                vmem((sz, sy // 2, 256, 2 * sx), BF16),
                vmem((sy // 2, 64, sx), F32),
                vmem((8, 128, 256), BF16),
                vmem((256, 256), BF16),
                vmem((192, 288), BF16),
                vmem((96, 576), BF16),
                vmem((256, 256), F32),
                vmem((288, 256), F32),
                vmem((32 * rows, sx), F32),
                vmem((32 * rows, sx), F32),
                vmem((32 * rows, sx), BF16),
                vmem((32 * rows, sx), BF16),
                vmem((2, 8, 32, 128), F32),
                vmem((8, 32, 128), F32),
                vmem((8, 32, 128), F32),
                vmem((max(nz - 1, 1), 32, 128), F32),
                vmem((32, 128), F32),
                vmem((plane, 32, 128), F32),
                vmem((2, 8, 32, 128), F32),
                vmem((1, 128, 128), F32),
                vmem((32, 128), F32),
                vmem((32, 128), F32),
                vmem((nz, 16, 128), F32),
                vmem((2, 16, 128), F32),
                vmem((plane, 16, 128), F32),
                vmem((2, 16, 128), F32),
                dma((3,)), dma((2,)), dma((2,)),
                dma((3, 8)), dma((3, 8)),
                dma((4,)), dma((4,)),
                dma((3, nz - 1)), dma((3, nz - 1)),
                dma((2, plane - 1)), dma((2, plane - 1)),
            ],
            compiler_params=pltpu.CompilerParams(
                collective_id=0, has_side_effects=True, vmem_limit_bytes=48 * 2**20
            ),
        )(vol, one, two, cot)
        g_one = g_one.reshape(3, 3, 3, 4, 32).transpose(4, 3, 0, 1, 2)
        g_two = g_two.reshape(3, 3, 3, 32, 64).transpose(4, 3, 0, 1, 2)
        return acts.reshape(volumes.shape), grads.reshape(volumes.shape), g_one, g_two

    in_specs = (P("dp", None, "gz", "gy", None), P(), P(), P("dp", None, "gz", "gy", None))
    out_specs = (P("dp", None, "gz", "gy", None), P("dp", None, "gz", "gy", None), P(), P())
    return jax.shard_map(per_device, mesh=mesh, in_specs=in_specs, out_specs=out_specs, check_vma=False)
```

```python
import functools
import math

import jax
import jax.numpy as jnp
from jax import lax
from jax.experimental import pallas as pl
from jax.experimental.pallas import tpu as pltpu
from jax.sharding import PartitionSpec as P

LEAK = 0.3
REST = 1.0 - LEAK
LOG_TWO = math.log(2.0)
MESH = pl.DeviceIdType.MESH
F32 = jnp.float32
BF16 = jnp.bfloat16
LANES = 128
DIRS = tuple((dz, dy) for dz in (-1, 0, 1) for dy in (-1, 0, 1) if (dz, dy) != (0, 0))


def mm(a, b):
    return lax.dot_general(a, b, (((1,), (0,)), ((), ())), preferred_element_type=F32)


def mm_nt(a, b):
    return lax.dot_general(a, b, (((1,), (1,)), ((), ())), preferred_element_type=F32)


def eye(n, m):
    return (
        lax.broadcasted_iota(jnp.int32, (n, m), 0) == lax.broadcasted_iota(jnp.int32, (n, m), 1)
    ).astype(BF16)


def to_right(v):
    lane = lax.broadcasted_iota(jnp.int32, v.shape, 1)
    return jnp.where(lane == 0, 0.0, pltpu.roll(v, 1, axis=1))


def to_left(v):
    lane = lax.broadcasted_iota(jnp.int32, v.shape, 1)
    return jnp.where(lane == LANES - 1, 0.0, pltpu.roll(v, LANES - 1, axis=1))


def slope_of(v):
    return LEAK + REST / (1.0 + jnp.exp(-v))


def act_and_slope(v):
    e = jnp.exp(-jnp.abs(v))
    r = 1.0 / (1.0 + e)
    act = LEAK * v + REST * (jnp.maximum(v, 0.0) + jnp.log(1.0 + e) - LOG_TWO)
    return act, LEAK + REST * jnp.where(v >= 0.0, r, e * r)


def part(d, n):
    if d == 0:
        return pl.ds(1, n), pl.ds(1, n)
    if d == 1:
        return pl.ds(n, 1), pl.ds(0, 1)
    return pl.ds(1, 1), pl.ds(n + 1, 1)


def step_kernel(
    dims,
    vol, one_in, two_in, cot_in,
    acts_out, grads_out, one_out, two_out,
    one_ref, two_ref, cot_ref, cotf, raw, rawf, fine, pool, grad2, slope1, shifted, cots, sel, w1, w2, wb,
    sum1, sum2, flat1, flat2, half1, half2,
    ga, ra, sb, rb, sc, rc, fd,
    qa, qra, qs, qrb, qsc, qrc, qf,
    local_sem, out_ssem, out_rsem,
    h_ssem, h_rsem,
    pair_ssem, pair_rsem, line_ssem, line_rsem, plane_ssem, plane_rsem,
):
    nd, nz, ny, sz, sy, batch = dims
    rows = sz * sy
    core = lax.axis_index("pipe")
    iz, iy, idp = lax.axis_index("gz"), lax.axis_index("gy"), lax.axis_index("dp")
    other = 1 - core
    plane = nd * ny
    me_plane = idp * ny + iy

    def on_line(off):
        return lax.rem(iz + off, nz)

    def on_plane(off):
        q = lax.rem(me_plane + off, plane)
        return q, {"dp": q // ny, "gy": lax.rem(q, ny)}

    def exists(dz, dy):
        ok = jnp.bool_(True)
        if dz == 1:
            ok = jnp.logical_and(ok, iz < nz - 1)
        if dz == -1:
            ok = jnp.logical_and(ok, iz > 0)
        if dy == 1:
            ok = jnp.logical_and(ok, iy < ny - 1)
        if dy == -1:
            ok = jnp.logical_and(ok, iy > 0)
        return ok

    def neighbour(dz, dy):
        return {"gz": lax.rem(iz + dz + nz, nz), "gy": lax.rem(iy + dy + ny, ny)}

    def halo_copy(k, ref, d):
        dz, dy = DIRS[d]
        (fz, tz), (fy, ty) = part(dz, ref.shape[0] - 2), part(dy, ref.shape[1] - 2)
        return pltpu.make_async_remote_copy(
            src_ref=ref.at[fz, fy],
            dst_ref=ref.at[tz, ty],
            send_sem=h_ssem.at[k, d],
            recv_sem=h_rsem.at[k, d],
            device_id=neighbour(dz, dy),
            device_id_type=MESH,
        )

    def halo_clear(ref):
        for dz, dy in DIRS:
            _, tz = part(dz, ref.shape[0] - 2)
            _, ty = part(dy, ref.shape[1] - 2)

            @pl.when(jnp.logical_not(exists(-dz, -dy)))
            def _():
                view = ref.at[tz, ty]
                view[...] = jnp.zeros(view.shape, view.dtype)

    def halo_send(k, ref):
        for d, (dz, dy) in enumerate(DIRS):

            @pl.when(exists(dz, dy))
            def _():
                halo_copy(k, ref, d).start()

    def halo_arrive(k, ref):
        for d, (dz, dy) in enumerate(DIRS):

            @pl.when(exists(-dz, -dy))
            def _():
                halo_copy(k, ref, d).wait_recv()

    def halo_sent(k, ref):
        for d, (dz, dy) in enumerate(DIRS):

            @pl.when(exists(dz, dy))
            def _():
                halo_copy(k, ref, d).wait_send()

    def to_pair(k, src, dst):
        return pltpu.make_async_remote_copy(
            src_ref=src, dst_ref=dst, send_sem=pair_ssem.at[k], recv_sem=pair_rsem.at[k],
            device_id={"pipe": other}, device_id_type=MESH,
        )

    def to_line(k, off, src, dst):
        return pltpu.make_async_remote_copy(
            src_ref=src, dst_ref=dst, send_sem=line_ssem.at[k, off - 1], recv_sem=line_rsem.at[k, off - 1],
            device_id={"gz": on_line(off)}, device_id_type=MESH,
        )

    def to_plane(k, off, src, dst):
        return pltpu.make_async_remote_copy(
            src_ref=src, dst_ref=dst, send_sem=plane_ssem.at[k, off - 1], recv_sem=plane_rsem.at[k, off - 1],
            device_id=on_plane(off)[1], device_id_type=MESH,
        )

    fetch = pltpu.make_async_copy(vol.at[core], raw, local_sem.at[0])
    fetch.start()
    fetch_more = [
        pltpu.make_async_copy(src, dst, local_sem.at[3 + k])
        for k, (src, dst) in enumerate(((one_in, one_ref), (two_in, two_ref), (cot_in.at[core], cot_ref)))
    ]
    for copy in fetch_more:
        copy.start()
    barrier = pltpu.get_barrier_semaphore()
    pl.semaphore_signal(barrier, inc=1, device_id={"pipe": other}, device_id_type=MESH)
    count = jnp.int32(1 + (nz - 1) + (plane - 1))
    for dz, dy in DIRS:
        if dz != 0 and dy != 0:

            @pl.when(exists(dz, dy))
            def _():
                pl.semaphore_signal(barrier, inc=1, device_id=neighbour(dz, dy), device_id_type=MESH)

            count = count + exists(dz, dy).astype(jnp.int32)
    for off in range(1, plane):
        pl.semaphore_signal(barrier, inc=1, device_id=on_plane(off)[1], device_id_type=MESH)
    for off in range(1, nz):
        pl.semaphore_signal(barrier, inc=1, device_id={"gz": on_line(off)}, device_id_type=MESH)

    halo_clear(fine)
    halo_clear(pool)
    halo_clear(grad2)

    fetch.wait()
    rawf[...] = raw[...].astype(F32)

    def spread_row(z, y):
        t = rawf[pl.ds(z * sy + y, 32, stride=rows), :]
        sub = lax.broadcasted_iota(jnp.int32, t.shape, 0)
        odd = (sub & 4) != 0
        low = jnp.where(odd, to_right(t), t)
        high = jnp.where(odd, t, to_left(t))
        for a in range(2):
            for b in range(2):
                j = 8 * (2 * a + b)
                both = jnp.concatenate([low[j : j + 8], high[j : j + 8]], axis=0)
                fine[2 * z + a + 1, 2 * y + b + 1] = both.astype(BF16)

    def loop_rows(body):
        def outer(z, _):
            def inner(y, __):
                body(z, y)
                return 0

            lax.fori_loop(0, sy, inner, 0, unroll=4)
            return 0

        lax.fori_loop(0, sz, outer, 0)

    def loop_pairs(z, body):
        def inner(p, _):
            body(z, p)
            return 0

        lax.fori_loop(0, sy // 2, inner, 0, unroll=True)

    loop_rows(spread_row)
    pl.semaphore_wait(barrier, count)
    halo_send(0, fine)

    for copy in fetch_more:
        copy.wait()
    row = lax.broadcasted_iota(jnp.int32, (128, 256), 0)
    lane = lax.broadcasted_iota(jnp.int32, (128, 256), 1)
    tap = row >> 2
    by3 = (tap * 11) >> 5
    by9 = (by3 * 11) >> 5
    tx, ty, tz = tap - 3 * by3, by3 - 3 * by9, by9
    for d in range(27):
        qa[0, 4 * d : 4 * d + 4, 0:32] = one_ref[d].astype(F32)
    qa[0, 108:128, 0:32] = jnp.zeros((20, 32), F32)
    one_t = mm_nt(eye(32, 32), qa[0, :, 0:32].astype(BF16)).astype(BF16)
    for s in range(8):
        a, b, c = s >> 2, (s >> 1) & 1, s & 1
        fx = tx + c
        slot = fx + 1 - 2 * (fx & 1)
        target = (tz + a) * 64 + (ty + b) * 16 + slot * 4 + (row & 3)
        hit = jnp.logical_and(lane == target, row < 108)
        sel[s] = jnp.where(hit, 1.0, 0.0).astype(BF16)
        w1[32 * s : 32 * s + 32, :] = mm(one_t, sel[s]).astype(BF16)
    for dx in range(3):
        taps = jnp.concatenate([two_ref[3 * j + dx] for j in range(9)], axis=0)
        w2[64 * dx : 64 * dx + 64, :] = mm_nt(eye(64, 64), taps).astype(BF16)
    for ex in range(3):
        blocks = [two_ref[3 * (8 - j) + 2 - ex].astype(F32) for j in range(9)]
        for j in range(0, 8, 2):
            pair = jnp.concatenate([blocks[j], blocks[j + 1]], axis=1)
            wb[32 * ex : 32 * ex + 32, 64 * j : 64 * j + 128] = pair.astype(BF16)
        wb[32 * ex : 32 * ex + 32, 512:576] = blocks[8].astype(BF16)
    double = (
        (lax.broadcasted_iota(jnp.int32, (64, LANES), 1) >> 1)
        == lax.broadcasted_iota(jnp.int32, (64, LANES), 0)
    ).astype(BF16)
    for o in range(64):
        cotf[4 * o : 4 * o + 4, 0:64] = cot_ref[o].astype(F32)
    for y in range(sy // 2):
        mine = cotf[pl.ds(y, 64, stride=sy // 2), :]
        cots[y] = mm(mine[:, 0:64].astype(BF16), double) * 0.125

    def windows(z, p):
        return jnp.concatenate(
            [fine[pl.ds(2 * z, 4), pl.ds(4 * p + 2 * j, 4)].reshape(256, LANES) for j in range(2)], axis=1
        )

    def first_pair(z, p):
        pre = mm(w1[...], windows(z, p))
        for j in range(2):
            y = 2 * p + j
            total = jnp.zeros((32, LANES), F32)
            for s in range(8):
                act, slope = act_and_slope(pre[32 * s : 32 * s + 32, LANES * j : LANES * j + LANES])
                total = total + act
                slope1[z, y, 32 * s : 32 * s + 32, :] = slope
            mean = total * 0.125
            pool[z + 1, y + 1] = mean.astype(BF16)
            flat1[pl.ds(z * sy + y, 32, stride=rows), :] = mean

    halo_arrive(0, fine)
    for z in range(sz):
        loop_pairs(z, first_pair)
    halo_send(1, pool)
    half1[...] = flat1[...].astype(BF16)

    def out_copies(k, half, out):
        here = pltpu.make_async_copy(half, out.at[core], local_sem.at[1 + k])
        there = pltpu.make_async_remote_copy(
            src_ref=half, dst_ref=out.at[core], send_sem=out_ssem.at[k], recv_sem=out_rsem.at[k],
            device_id={"pipe": other}, device_id_type=MESH,
        )
        return here, there

    for copy in out_copies(0, half1, acts_out):
        copy.start()

    def second_pair(z, p):
        cells = jnp.concatenate(
            [pool[pl.ds(z, 3), pl.ds(2 * p + j, 3)].reshape(288, LANES) for j in range(2)], axis=1
        )
        prod = mm(w2[...], cells)
        for j in range(2):
            mine = prod[:, LANES * j : LANES * j + LANES]
            pre = to_right(mine[0:64]) + mine[64:128] + to_left(mine[128:192])
            g = (slope_of(pre) * cots[p]).astype(BF16)
            grad2[z + 1, 2 * p + j + 1] = g
            wide = g.astype(F32)
            right = to_right(wide).astype(BF16)
            cols = slice(LANES * j, LANES * j + LANES)
            shifted[z, p, 0:64, cols] = to_left(wide).astype(BF16)
            shifted[z, p, 64:128, cols] = g
            shifted[z, p, 128:192, cols] = right
            shifted[z, p, 192:256, cols] = right

    halo_arrive(1, pool)
    for z in range(sz):
        loop_pairs(z, second_pair)
    halo_send(2, grad2)

    sum2[...] = jnp.zeros(sum2.shape, F32)

    def second_terms(z, p):
        cells = jnp.concatenate(
            [pool[pl.ds(z, 3), pl.ds(2 * p + j, 3)].reshape(288, LANES) for j in range(2)], axis=1
        )
        sum2[...] += mm_nt(cells, shifted[z, p])

    for z in range(sz):
        loop_pairs(z, second_terms)
    for r in range(9):
        ga[r // 8, r % 8] = sum2[32 * r : 32 * r + 32, 0:128]
    keep = lax.broadcasted_iota(jnp.int32, (16, LANES), 1) < 64
    for r in range(9):
        lo, hi = sum2[16 * r : 16 * r + 16, 128:256], sum2[144 + 16 * r : 160 + 16 * r, 128:256]
        at = 288 + 16 * r
        ga[at // 256, at % 256 // 32, at % 32 : at % 32 + 16] = jnp.where(keep, lo, hi)
    ga[1, 5, 16:32] = jnp.zeros((16, LANES), F32)
    ga[1, 6] = jnp.zeros((32, LANES), F32)
    ga[1, 7] = jnp.zeros((32, LANES), F32)
    to_pair(0, ga.at[other], ra).start()

    sum1[...] = jnp.zeros(sum1.shape, F32)

    def back_pair(z, p):
        cells = jnp.concatenate(
            [grad2[pl.ds(z, 3), pl.ds(2 * p + j, 3)].reshape(576, LANES) for j in range(2)], axis=1
        )
        prod = mm(wb[...], cells)
        grads = []
        for j in range(2):
            y = 2 * p + j
            mine = prod[:, LANES * j : LANES * j + LANES]
            back = to_right(mine[0:32]) + mine[32:64] + to_left(mine[64:96])
            back = back.astype(BF16).astype(F32)
            flat2[pl.ds(z * sy + y, 32, stride=rows), :] = back
            eighth = back * 0.125
            grads.append(
                jnp.concatenate(
                    [(slope1[z, y, 32 * s : 32 * s + 32, :] * eighth).astype(BF16) for s in range(8)], axis=0
                )
            )
        sum1[...] += mm_nt(jnp.concatenate(grads, axis=1), windows(z, p))

    line = range(1, nz)
    flat = range(1, plane)

    halo_arrive(2, grad2)
    loop_pairs(0, back_pair)
    to_pair(0, ga.at[other], ra).wait_recv()
    for j in range(8):
        sb[j] = ga[core, j] + ra[j]
    for off in line:
        to_line(0, off, sb.at[on_line(off)], rb.at[off - 1]).start()
    for z in range(1, sz):
        loop_pairs(z, back_pair)

    folded = jnp.zeros((32, LANES), F32)
    for s in range(8):
        mine = sum1[32 * s : 32 * s + 32, :]
        high = mine.astype(BF16)
        low = (mine - high.astype(F32)).astype(BF16)
        folded = folded + mm_nt(high, sel[s]) + mm_nt(low, sel[s])
    qs[...] = folded
    to_pair(1, qs, qra).start()
    half2[...] = flat2[...].astype(BF16)
    for copy in out_copies(1, half2, grads_out):
        copy.start()

    for off in line:
        to_line(0, off, sb.at[on_line(off)], rb.at[off - 1]).wait_recv()
    total = sb[iz]
    for off in line:
        total = total + rb[off - 1]
    sc[...] = total
    rc[me_plane] = total
    for off in flat:
        to_plane(0, off, sc, rc.at[me_plane]).start()

    to_pair(1, qs, qra).wait_recv()
    both = qs[...] + qra[...]
    mine = jnp.where(core == 0, both[0:16], both[16:32])
    qsc[0] = mine
    qrb[iz] = mine
    for off in line:
        to_line(1, off, qsc.at[0], qrb.at[iz]).start()

    for off in flat:
        to_plane(0, off, sc, rc.at[me_plane]).wait_recv()
    total = rc[0]
    for q in range(1, plane):
        total = total + rc[q]
    fd[core, iz] = total * (1.0 / batch)
    for off in line:
        to_line(2, off, fd.at[core, iz], fd.at[core, iz]).start()

    for off in line:
        to_line(1, off, qsc.at[0], qrb.at[iz]).wait_recv()
    total = qrb[0]
    for q in range(1, nz):
        total = total + qrb[q]
    qsc[1] = total
    qrc[me_plane] = total
    for off in flat:
        to_plane(1, off, qsc.at[1], qrc.at[me_plane]).start()

    for off in line:
        to_line(2, off, fd.at[core, iz], fd.at[core, iz]).wait_recv()
    to_pair(2, fd.at[core], fd.at[core]).start()

    for off in flat:
        to_plane(1, off, qsc.at[1], qrc.at[me_plane]).wait_recv()
    total = qrc[0]
    for q in range(1, plane):
        total = total + qrc[q]
    qf[core] = total * (1.0 / batch)
    to_pair(3, qf.at[core], qf.at[core]).start()

    to_pair(2, fd.at[core], fd.at[core]).wait_recv()
    for j in range(9):
        block = fd[j // 8, j % 8]
        two_out[3 * j] = block[:, 0:64]
        two_out[3 * j + 1] = pltpu.roll(block, 64, axis=1)[:, 0:64]
    for r in range(9):
        at = 288 + 16 * r
        block = fd[at // 256, at % 256 // 32, at % 32 : at % 32 + 16]
        for first, values in ((16 * r, block), (144 + 16 * r, pltpu.roll(block, 64, axis=1))):
            two_out[3 * (first // 32) + 2, first % 32 : first % 32 + 16, :] = values[:, 0:64]
    to_pair(3, qf.at[core], qf.at[core]).wait_recv()
    turned = jnp.transpose(jnp.concatenate([qf[0], qf[1]], axis=0))
    for d in range(27):
        one_out[d] = turned[4 * d : 4 * d + 4, :]

    for k, ref in enumerate((fine, pool, grad2)):
        halo_sent(k, ref)
    to_pair(0, ga.at[other], ra).wait_send()
    to_pair(1, qs, qra).wait_send()
    to_pair(2, fd.at[core], fd.at[core]).wait_send()
    to_pair(3, qf.at[core], qf.at[core]).wait_send()
    for off in line:
        to_line(0, off, sb.at[on_line(off)], rb.at[off - 1]).wait_send()
        to_line(1, off, qsc.at[0], qrb.at[iz]).wait_send()
        to_line(2, off, fd.at[core, iz], fd.at[core, iz]).wait_send()
    for off in flat:
        to_plane(0, off, sc, rc.at[me_plane]).wait_send()
        to_plane(1, off, qsc.at[1], qrc.at[me_plane]).wait_send()
    for k, (half, out) in enumerate(((half1, acts_out), (half2, grads_out))):
        here, there = out_copies(k, half, out)
        here.wait()
        there.wait()


def leave_kernel(*refs):
    sem = refs[8]
    copies = [pltpu.make_async_copy(refs[k], refs[4 + k], sem.at[k]) for k in range(4)]
    for copy in copies:
        copy.start()
    for copy in copies:
        copy.wait()


def solution(mesh):
    nd, nz, ny = mesh.shape["dp"], mesh.shape["gz"], mesh.shape["gy"]
    plane = nd * ny

    def per_device(volumes, conv_one, conv_two, cotangent):
        micro, feats, sz, sy, sx = volumes.shape
        rows = sz * sy
        dims = (nd, nz, ny, sz, sy, micro * nd)
        vol = volumes.reshape(micro, feats * rows, sx)
        one = conv_one.transpose(2, 3, 4, 1, 0).reshape(27, 4, 32)
        two = conv_two.transpose(2, 3, 4, 1, 0).reshape(27, 32, 64)
        cot = cotangent[:, :, 0]
        whole = pl.BlockSpec(memory_space=pltpu.VMEM)
        away = pl.BlockSpec(memory_space=pltpu.HBM)
        vmem = pltpu.VMEM
        dma = pltpu.SemaphoreType.DMA
        results = ((vol.shape, BF16), (vol.shape, BF16), ((27, 4, 32), F32), ((27, 32, 64), F32))
        held = pl.pallas_call(
            functools.partial(step_kernel, dims),
            out_shape=tuple(vmem(shape, dtype) for shape, dtype in results),
            in_specs=[away] * 4,
            out_specs=(whole,) * 4,
            scratch_shapes=[
                vmem((27, 4, 32), BF16),
                vmem((27, 32, 64), BF16),
                vmem((64, sy // 2, 64), BF16),
                vmem((64 * (sy // 2), LANES), F32),
                vmem((feats * rows, sx), BF16),
                vmem((feats * rows, sx), F32),
                vmem((2 * sz + 2, 2 * sy + 2, 16, sx), BF16),
                vmem((sz + 2, sy + 2, 32, sx), BF16),
                vmem((sz + 2, sy + 2, 64, sx), BF16),
                vmem((sz, sy, 256, sx), F32),
                vmem((sz, sy // 2, 256, 2 * sx), BF16),
                vmem((sy // 2, 64, sx), F32),
                vmem((8, 128, 256), BF16),
                vmem((256, 256), BF16),
                vmem((192, 288), BF16),
                vmem((96, 576), BF16),
                vmem((256, 256), F32),
                vmem((288, 256), F32),
                vmem((32 * rows, sx), F32),
                vmem((32 * rows, sx), F32),
                vmem((32 * rows, sx), BF16),
                vmem((32 * rows, sx), BF16),
                vmem((2, 8, 32, 128), F32),
                vmem((8, 32, 128), F32),
                vmem((8, 32, 128), F32),
                vmem((max(nz - 1, 1), 32, 128), F32),
                vmem((32, 128), F32),
                vmem((plane, 32, 128), F32),
                vmem((2, 8, 32, 128), F32),
                vmem((1, 128, 128), F32),
                vmem((32, 128), F32),
                vmem((32, 128), F32),
                vmem((nz, 16, 128), F32),
                vmem((2, 16, 128), F32),
                vmem((plane, 16, 128), F32),
                vmem((2, 16, 128), F32),
                dma((6,)), dma((2,)), dma((2,)),
                dma((3, 8)), dma((3, 8)),
                dma((4,)), dma((4,)),
                dma((3, nz - 1)), dma((3, nz - 1)),
                dma((2, plane - 1)), dma((2, plane - 1)),
            ],
            compiler_params=pltpu.CompilerParams(
                collective_id=0, has_side_effects=True, vmem_limit_bytes=48 * 2**20
            ),
        )(*(pltpu.with_memory_space_constraint(a, pltpu.HBM) for a in (vol, one, two, cot)))
        acts, grads, g_one, g_two = pl.pallas_call(
            leave_kernel,
            out_shape=tuple(jax.ShapeDtypeStruct(shape, dtype) for shape, dtype in results),
            in_specs=[whole] * 4,
            out_specs=(away,) * 4,
            scratch_shapes=[dma((4,))],
        )(*(pltpu.with_memory_space_constraint(a, pltpu.VMEM) for a in held))
        g_one = g_one.reshape(3, 3, 3, 4, 32).transpose(4, 3, 0, 1, 2)
        g_two = g_two.reshape(3, 3, 3, 32, 64).transpose(4, 3, 0, 1, 2)
        return acts.reshape(volumes.shape), grads.reshape(volumes.shape), g_one, g_two

    in_specs = (P("dp", None, "gz", "gy", None), P(), P(), P("dp", None, "gz", "gy", None))
    out_specs = (P("dp", None, "gz", "gy", None), P("dp", None, "gz", "gy", None), P(), P())
    return jax.shard_map(per_device, mesh=mesh, in_specs=in_specs, out_specs=out_specs, check_vma=False)
```

```python
import functools
import math

import jax
import jax.numpy as jnp
from jax import lax
from jax.experimental import pallas as pl
from jax.experimental.pallas import tpu as pltpu
from jax.sharding import PartitionSpec as P

LEAK = 0.3
REST = 1.0 - LEAK
LOG_TWO = math.log(2.0)
MESH = pl.DeviceIdType.MESH
F32 = jnp.float32
BF16 = jnp.bfloat16
LANES = 128
DIRS = tuple((dz, dy) for dz in (-1, 0, 1) for dy in (-1, 0, 1) if (dz, dy) != (0, 0))


def mm(a, b):
    return lax.dot_general(a, b, (((1,), (0,)), ((), ())), preferred_element_type=F32)


def mm_nt(a, b):
    return lax.dot_general(a, b, (((1,), (1,)), ((), ())), preferred_element_type=F32)


def eye(n, m):
    return (
        lax.broadcasted_iota(jnp.int32, (n, m), 0) == lax.broadcasted_iota(jnp.int32, (n, m), 1)
    ).astype(BF16)


def to_right(v):
    lane = lax.broadcasted_iota(jnp.int32, v.shape, 1)
    return jnp.where(lane == 0, 0.0, pltpu.roll(v, 1, axis=1))


def to_left(v):
    lane = lax.broadcasted_iota(jnp.int32, v.shape, 1)
    return jnp.where(lane == LANES - 1, 0.0, pltpu.roll(v, LANES - 1, axis=1))


def slope_of(v):
    return (LEAK + 0.5 * REST) + (0.5 * REST) * jnp.tanh(0.5 * v)


def part(d, n):
    if d == 0:
        return pl.ds(1, n), pl.ds(1, n)
    if d == 1:
        return pl.ds(n, 1), pl.ds(0, 1)
    return pl.ds(1, 1), pl.ds(n + 1, 1)


def step_kernel(
    dims,
    vol, one_in, two_in, cot_in,
    acts_out, grads_out, one_out, two_out,
    one_ref, two_ref, cot_ref, cotf, raw, rawf, fine, pool, grad2, slope1, shifted, cots, sel, w1, w2, wb,
    sum1, sum2, flat1, flat2, half1, half2,
    ga, ra, sb, rb, sc, rc, fd,
    qa, qra, qs, qrb, qsc, qrc, qf,
    local_sem, out_ssem, out_rsem,
    h_ssem, h_rsem,
    word_sem, pair_ssem, pair_rsem, line_ssem, line_rsem, plane_ssem, plane_rsem,
):
    nd, nz, ny, sz, sy, batch = dims
    rows = sz * sy
    core = lax.axis_index("pipe")
    iz, iy, idp = lax.axis_index("gz"), lax.axis_index("gy"), lax.axis_index("dp")
    other = 1 - core
    plane = nd * ny
    me_plane = idp * ny + iy

    def on_line(off):
        return lax.rem(iz + off, nz)

    def on_plane(off):
        q = lax.rem(me_plane + off, plane)
        return q, {"dp": q // ny, "gy": lax.rem(q, ny)}

    def exists(dz, dy):
        ok = jnp.bool_(True)
        if dz == 1:
            ok = jnp.logical_and(ok, iz < nz - 1)
        if dz == -1:
            ok = jnp.logical_and(ok, iz > 0)
        if dy == 1:
            ok = jnp.logical_and(ok, iy < ny - 1)
        if dy == -1:
            ok = jnp.logical_and(ok, iy > 0)
        return ok

    def neighbour(dz, dy):
        return {"gz": lax.rem(iz + dz + nz, nz), "gy": lax.rem(iy + dy + ny, ny)}

    def halo_copy(k, ref, d):
        dz, dy = DIRS[d]
        (fz, tz), (fy, ty) = part(dz, ref.shape[0] - 2), part(dy, ref.shape[1] - 2)
        return pltpu.make_async_remote_copy(
            src_ref=ref.at[fz, fy],
            dst_ref=ref.at[tz, ty],
            send_sem=h_ssem.at[k, d],
            recv_sem=h_rsem.at[k, d],
            device_id=neighbour(dz, dy),
            device_id_type=MESH,
        )

    turns = tuple(
        (p, dz, dy)
        for p in range(sz)
        for dz in (-1, 0, 1)
        for dy in (-1, 0, 1)
        if (dz, dy) != (0, 0) and (dz == 0 or p == (0 if dz == -1 else sz - 1))
    )

    def plane_copy(k, ref, m):
        p, dz, dy = turns[m]
        fy, ty = part(dy, ref.shape[1] - 2)
        to_z = p + 1 if dz == 0 else (0 if dz == 1 else sz + 1)
        return pltpu.make_async_remote_copy(
            src_ref=ref.at[p + 1, fy],
            dst_ref=ref.at[to_z, ty],
            send_sem=h_ssem.at[k, m],
            recv_sem=h_rsem.at[k, m],
            device_id=neighbour(dz, dy),
            device_id_type=MESH,
        )

    def plane_send(k, ref, p):
        for m, (q, dz, dy) in enumerate(turns):
            if q == p:

                @pl.when(exists(dz, dy))
                def _():
                    plane_copy(k, ref, m).start()

    def plane_arrive(k, ref, wanted):
        for m, (q, dz, dy) in enumerate(turns):
            if dz in wanted:

                @pl.when(exists(-dz, -dy))
                def _():
                    plane_copy(k, ref, m).wait_recv()

    def planes_sent(k, ref):
        for m, (q, dz, dy) in enumerate(turns):

            @pl.when(exists(dz, dy))
            def _():
                plane_copy(k, ref, m).wait_send()

    def halo_clear(ref):
        for dz, dy in DIRS:
            _, tz = part(dz, ref.shape[0] - 2)
            _, ty = part(dy, ref.shape[1] - 2)

            @pl.when(jnp.logical_not(exists(-dz, -dy)))
            def _():
                view = ref.at[tz, ty]
                view[...] = jnp.zeros(view.shape, view.dtype)

    def halo_send(k, ref):
        for d, (dz, dy) in enumerate(DIRS):

            @pl.when(exists(dz, dy))
            def _():
                halo_copy(k, ref, d).start()

    def halo_arrive(k, ref):
        for d, (dz, dy) in enumerate(DIRS):

            @pl.when(exists(-dz, -dy))
            def _():
                halo_copy(k, ref, d).wait_recv()

    def halo_sent(k, ref):
        for d, (dz, dy) in enumerate(DIRS):

            @pl.when(exists(dz, dy))
            def _():
                halo_copy(k, ref, d).wait_send()

    def to_pair(k, src, dst):
        return pltpu.make_async_remote_copy(
            src_ref=src, dst_ref=dst, send_sem=pair_ssem.at[k], recv_sem=pair_rsem.at[k],
            device_id={"pipe": other}, device_id_type=MESH,
        )

    def to_line(k, off, src, dst):
        return pltpu.make_async_remote_copy(
            src_ref=src, dst_ref=dst, send_sem=line_ssem.at[k, off - 1], recv_sem=line_rsem.at[k, off - 1],
            device_id={"gz": on_line(off)}, device_id_type=MESH,
        )

    def to_plane(k, off, src, dst):
        return pltpu.make_async_remote_copy(
            src_ref=src, dst_ref=dst, send_sem=plane_ssem.at[k, off - 1], recv_sem=plane_rsem.at[k, off - 1],
            device_id=on_plane(off)[1], device_id_type=MESH,
        )

    fetch = pltpu.make_async_copy(vol.at[core], raw, local_sem.at[0])
    fetch.start()
    fetch_more = [
        pltpu.make_async_copy(src, dst, local_sem.at[3 + k])
        for k, (src, dst) in enumerate(((one_in, one_ref), (two_in, two_ref), (cot_in.at[core], cot_ref)))
    ]
    for copy in fetch_more:
        copy.start()
    barrier = pltpu.get_barrier_semaphore()
    pl.semaphore_signal(barrier, inc=1, device_id={"pipe": other}, device_id_type=MESH)
    near = [
        {axis: lax.rem(at + step, size)}
        for axis, at, size in (("gz", iz, nz), ("gy", iy, ny), ("dp", idp, nd))
        for step in (1, size - 1)
    ]
    count = jnp.int32(1 + len(near))
    for there in near:
        pl.semaphore_signal(barrier, inc=1, device_id=there, device_id_type=MESH)
    for dz, dy in DIRS:
        if dz != 0 and dy != 0:

            @pl.when(exists(dz, dy))
            def _():
                pl.semaphore_signal(barrier, inc=1, device_id=neighbour(dz, dy), device_id_type=MESH)

            count = count + exists(dz, dy).astype(jnp.int32)

    def spread_word(r):
        for there in near:
            pl.semaphore_signal(word_sem.at[r], inc=1, device_id=there, device_id_type=MESH)

    def hear_word(r):
        pl.semaphore_wait(word_sem.at[r], len(near))

    halo_clear(fine)
    halo_clear(pool)
    halo_clear(grad2)

    fetch.wait()
    rawf[...] = raw[...].astype(F32)

    def spread_row(z, y):
        t = rawf[pl.ds(z * sy + y, 32, stride=rows), :]
        sub = lax.broadcasted_iota(jnp.int32, t.shape, 0)
        odd = (sub & 4) != 0
        low = jnp.where(odd, to_right(t), t)
        high = jnp.where(odd, t, to_left(t))
        for a in range(2):
            for b in range(2):
                j = 8 * (2 * a + b)
                both = jnp.concatenate([low[j : j + 8], high[j : j + 8]], axis=0)
                fine[2 * z + a + 1, 2 * y + b + 1] = both.astype(BF16)

    def loop_rows(body):
        def outer(z, _):
            def inner(y, __):
                body(z, y)
                return 0

            lax.fori_loop(0, sy, inner, 0, unroll=4)
            return 0

        lax.fori_loop(0, sz, outer, 0)

    def loop_pairs(z, body, first=0, last=sy // 2):
        for p in range(first, last):
            body(z, p)

    up, down = tuple(range(sz)), tuple(reversed(range(sz)))

    def needs(order, z):
        wanted = () if z != order[0] else (0,)
        if z == 0:
            wanted += (1,)
        if z == sz - 1:
            wanted += (-1,)
        return wanted

    loop_rows(spread_row)
    pl.semaphore_wait(barrier, count)
    halo_send(0, fine)
    spread_word(0)

    for copy in fetch_more:
        copy.wait()
    row = lax.broadcasted_iota(jnp.int32, (128, 256), 0)
    lane = lax.broadcasted_iota(jnp.int32, (128, 256), 1)
    tap = row >> 2
    by3 = (tap * 11) >> 5
    by9 = (by3 * 11) >> 5
    tx, ty, tz = tap - 3 * by3, by3 - 3 * by9, by9
    for d in range(27):
        qa[0, 4 * d : 4 * d + 4, 0:32] = one_ref[d].astype(F32)
    qa[0, 108:128, 0:32] = jnp.zeros((20, 32), F32)
    one_t = mm_nt(eye(32, 32), qa[0, :, 0:32].astype(BF16)).astype(BF16)
    for s in range(8):
        a, b, c = s >> 2, (s >> 1) & 1, s & 1
        fx = tx + c
        slot = fx + 1 - 2 * (fx & 1)
        target = (tz + a) * 64 + (ty + b) * 16 + slot * 4 + (row & 3)
        hit = jnp.logical_and(lane == target, row < 108)
        sel[s] = jnp.where(hit, 1.0, 0.0).astype(BF16)
        w1[32 * s : 32 * s + 32, :] = mm(one_t, sel[s]).astype(BF16)
    for dx in range(3):
        taps = jnp.concatenate([two_ref[3 * j + dx] for j in range(9)], axis=0)
        w2[64 * dx : 64 * dx + 64, :] = mm_nt(eye(64, 64), taps).astype(BF16)
    for ex in range(3):
        blocks = [two_ref[3 * (8 - j) + 2 - ex].astype(F32) for j in range(9)]
        for j in range(0, 8, 2):
            pair = jnp.concatenate([blocks[j], blocks[j + 1]], axis=1)
            wb[32 * ex : 32 * ex + 32, 64 * j : 64 * j + 128] = pair.astype(BF16)
        wb[32 * ex : 32 * ex + 32, 512:576] = blocks[8].astype(BF16)
    double = (
        (lax.broadcasted_iota(jnp.int32, (64, LANES), 1) >> 1)
        == lax.broadcasted_iota(jnp.int32, (64, LANES), 0)
    ).astype(BF16)
    for o in range(64):
        cotf[4 * o : 4 * o + 4, 0:64] = cot_ref[o].astype(F32)
    for y in range(sy // 2):
        mine = cotf[pl.ds(y, 64, stride=sy // 2), :]
        cots[y] = mm(mine[:, 0:64].astype(BF16), double) * 0.125

    def windows(z, p):
        return jnp.concatenate(
            [fine[pl.ds(2 * z, 4), pl.ds(4 * p + 2 * j, 4)].reshape(256, LANES) for j in range(2)], axis=1
        )

    def first_pair(z, p):
        pre = mm(w1[...], windows(z, p))
        for j in range(2):
            y = 2 * p + j
            straight, product = None, None
            for s in range(8):
                v = pre[32 * s : 32 * s + 32, LANES * j : LANES * j + LANES]
                slope1[z, y, 32 * s : 32 * s + 32, :] = slope_of(v)
                bend, grown = jnp.maximum(v, LEAK * v), 1.0 + jnp.exp(-jnp.abs(v))
                straight = bend if s == 0 else straight + bend
                product = grown if s == 0 else product * grown
            mean = 0.125 * straight + (0.125 * REST) * jnp.log(product) - REST * LOG_TWO
            pool[z + 1, y + 1] = mean.astype(BF16)
            flat1[pl.ds(z * sy + y, 32, stride=rows), :] = mean

    hear_word(0)
    spread_word(1)
    halo_arrive(0, fine)
    for z in up:
        loop_pairs(z, first_pair)
        plane_send(1, pool, z)
    hear_word(1)
    spread_word(2)
    half1[...] = flat1[...].astype(BF16)

    def out_copies(k, half, out):
        here = pltpu.make_async_copy(half, out.at[core], local_sem.at[1 + k])
        there = pltpu.make_async_remote_copy(
            src_ref=half, dst_ref=out.at[core], send_sem=out_ssem.at[k], recv_sem=out_rsem.at[k],
            device_id={"pipe": other}, device_id_type=MESH,
        )
        return here, there

    for copy in out_copies(0, half1, acts_out):
        copy.start()

    def second_pair(z, p):
        cells = jnp.concatenate(
            [pool[pl.ds(z, 3), pl.ds(2 * p + j, 3)].reshape(288, LANES) for j in range(2)], axis=1
        )
        prod = mm(w2[...], cells)
        for j in range(2):
            mine = prod[:, LANES * j : LANES * j + LANES]
            pre = to_right(mine[0:64]) + mine[64:128] + to_left(mine[128:192])
            g = (slope_of(pre) * cots[p]).astype(BF16)
            grad2[z + 1, 2 * p + j + 1] = g
            wide = g.astype(F32)
            right = to_right(wide).astype(BF16)
            cols = slice(LANES * j, LANES * j + LANES)
            shifted[z, p, 0:64, cols] = to_left(wide).astype(BF16)
            shifted[z, p, 64:128, cols] = g
            shifted[z, p, 128:192, cols] = right
            shifted[z, p, 192:256, cols] = right

    for z in down:
        plane_arrive(1, pool, needs(down, z))
        loop_pairs(z, second_pair)
        plane_send(2, grad2, z)

    sum2[...] = jnp.zeros(sum2.shape, F32)

    def second_terms(z, p):
        cells = jnp.concatenate(
            [pool[pl.ds(z, 3), pl.ds(2 * p + j, 3)].reshape(288, LANES) for j in range(2)], axis=1
        )
        sum2[...] += mm_nt(cells, shifted[z, p])

    for z in range(sz):
        loop_pairs(z, second_terms)
    for r in range(18):
        ga[r // 16, r % 16] = sum2[16 * r : 16 * r + 16, 0:128]
    keep = lax.broadcasted_iota(jnp.int32, (16, LANES), 1) < 64
    for r in range(9):
        lo, hi = sum2[16 * r : 16 * r + 16, 128:256], sum2[144 + 16 * r : 160 + 16 * r, 128:256]
        ga[1, 2 + r] = jnp.where(keep, lo, hi)
    for r in range(11, 16):
        ga[1, r] = jnp.zeros((16, LANES), F32)
    to_pair(0, ga.at[other], ra).start()

    sum1[...] = jnp.zeros(sum1.shape, F32)

    def back_pair(z, p):
        cells = jnp.concatenate(
            [grad2[pl.ds(z, 3), pl.ds(2 * p + j, 3)].reshape(576, LANES) for j in range(2)], axis=1
        )
        prod = mm(wb[...], cells)
        grads = []
        for j in range(2):
            y = 2 * p + j
            mine = prod[:, LANES * j : LANES * j + LANES]
            back = to_right(mine[0:32]) + mine[32:64] + to_left(mine[64:96])
            back = back.astype(BF16).astype(F32)
            flat2[pl.ds(z * sy + y, 32, stride=rows), :] = back
            eighth = back * 0.125
            grads.append(
                jnp.concatenate(
                    [(slope1[z, y, 32 * s : 32 * s + 32, :] * eighth).astype(BF16) for s in range(8)], axis=0
                )
            )
        sum1[...] += mm_nt(jnp.concatenate(grads, axis=1), windows(z, p))

    line = range(1, nz)
    flat = range(1, plane)

    hear_word(2)
    to_pair(0, ga.at[other], ra).wait_recv()
    sb[...] = ga[core] + ra[...]
    for off in flat:
        to_plane(0, off, sb.at[on_plane(off)[0]], rb.at[off - 1]).start()
    for z in up:
        plane_arrive(2, grad2, needs(up, z))
        loop_pairs(z, back_pair)

    pieces = []
    for s in range(8):
        mine = sum1[32 * s : 32 * s + 32, :]
        high = mine.astype(BF16)
        low = (mine - high.astype(F32)).astype(BF16)
        pieces.append(jnp.concatenate([high, low], axis=0))
    folded = mm_nt(jnp.concatenate(pieces, axis=1), jnp.concatenate([sel[s] for s in range(8)], axis=1))
    qs[...] = folded[0:32] + folded[32:64]
    to_pair(1, qs, qra).start()

    for off in flat:
        to_plane(0, off, sb.at[on_plane(off)[0]], rb.at[off - 1]).wait_recv()
    total = sb[me_plane]
    for off in flat:
        total = total + rb[off - 1]
    sc[...] = total
    rc[iz] = total
    for off in line:
        to_line(0, off, sc, rc.at[iz]).start()

    to_pair(1, qs, qra).wait_recv()
    both = qs[...] + qra[...]
    mine = jnp.where(core == 0, both[0:16], both[16:32])
    qsc[0] = mine
    qrc[me_plane] = mine
    for off in flat:
        to_plane(1, off, qsc.at[0], qrc.at[me_plane]).start()
    half2[...] = flat2[...].astype(BF16)
    for copy in out_copies(1, half2, grads_out):
        copy.start()

    for off in flat:
        to_plane(1, off, qsc.at[0], qrc.at[me_plane]).wait_recv()
    total = qrc[0]
    for q in range(1, plane):
        total = total + qrc[q]
    qsc[1] = total
    qrb[iz] = total
    for off in line:
        to_line(1, off, qsc.at[1], qrb.at[iz]).start()

    for off in line:
        to_line(0, off, sc, rc.at[iz]).wait_recv()
    total = rc[0]
    for q in range(1, nz):
        total = total + rc[q]
    fd[core, me_plane] = total * (1.0 / batch)
    for off in flat:
        to_plane(2, off, fd.at[core, me_plane], fd.at[core, me_plane]).start()

    for off in line:
        to_line(1, off, qsc.at[1], qrb.at[iz]).wait_recv()
    total = qrb[0]
    for q in range(1, nz):
        total = total + qrb[q]
    qf[core] = total * (1.0 / batch)
    to_pair(3, qf.at[core], qf.at[core]).start()

    for off in flat:
        to_plane(2, off, fd.at[core, me_plane], fd.at[core, me_plane]).wait_recv()
    to_pair(2, fd.at[core], fd.at[core]).start()

    to_pair(3, qf.at[core], qf.at[core]).wait_recv()
    turned = jnp.transpose(jnp.concatenate([qf[0], qf[1]], axis=0))
    for d in range(27):
        one_out[d] = turned[4 * d : 4 * d + 4, :]
    to_pair(2, fd.at[core], fd.at[core]).wait_recv()
    for j in range(18):
        block = fd[j // 16, j % 16]
        rows16 = slice(16 * (j % 2), 16 * (j % 2) + 16)
        two_out[3 * (j // 2), rows16, :] = block[:, 0:64]
        two_out[3 * (j // 2) + 1, rows16, :] = pltpu.roll(block, 64, axis=1)[:, 0:64]
    for r in range(9):
        block = fd[1, 2 + r]
        for first, values in ((16 * r, block), (144 + 16 * r, pltpu.roll(block, 64, axis=1))):
            two_out[3 * (first // 32) + 2, first % 32 : first % 32 + 16, :] = values[:, 0:64]

    halo_sent(0, fine)
    planes_sent(1, pool)
    planes_sent(2, grad2)
    to_pair(0, ga.at[other], ra).wait_send()
    to_pair(1, qs, qra).wait_send()
    to_pair(2, fd.at[core], fd.at[core]).wait_send()
    to_pair(3, qf.at[core], qf.at[core]).wait_send()
    for off in line:
        to_line(0, off, sc, rc.at[iz]).wait_send()
        to_line(1, off, qsc.at[1], qrb.at[iz]).wait_send()
    for off in flat:
        to_plane(0, off, sb.at[on_plane(off)[0]], rb.at[off - 1]).wait_send()
        to_plane(1, off, qsc.at[0], qrc.at[me_plane]).wait_send()
        to_plane(2, off, fd.at[core, me_plane], fd.at[core, me_plane]).wait_send()
    for k, (half, out) in enumerate(((half1, acts_out), (half2, grads_out))):
        here, there = out_copies(k, half, out)
        here.wait()
        there.wait()


def leave_kernel(*refs):
    sem = refs[8]
    copies = [pltpu.make_async_copy(refs[k], refs[4 + k], sem.at[k]) for k in range(4)]
    for copy in copies:
        copy.start()
    for copy in copies:
        copy.wait()


def solution(mesh):
    nd, nz, ny = mesh.shape["dp"], mesh.shape["gz"], mesh.shape["gy"]
    plane = nd * ny

    def per_device(volumes, conv_one, conv_two, cotangent):
        micro, feats, sz, sy, sx = volumes.shape
        rows = sz * sy
        dims = (nd, nz, ny, sz, sy, micro * nd)
        vol = volumes.reshape(micro, feats * rows, sx)
        one = conv_one.transpose(2, 3, 4, 1, 0).reshape(27, 4, 32)
        two = conv_two.transpose(2, 3, 4, 1, 0).reshape(27, 32, 64)
        cot = cotangent[:, :, 0]
        whole = pl.BlockSpec(memory_space=pltpu.VMEM)
        away = pl.BlockSpec(memory_space=pltpu.HBM)
        vmem = pltpu.VMEM
        dma = pltpu.SemaphoreType.DMA
        results = ((vol.shape, BF16), (vol.shape, BF16), ((27, 4, 32), F32), ((27, 32, 64), F32))
        held = pl.pallas_call(
            functools.partial(step_kernel, dims),
            out_shape=tuple(vmem(shape, dtype) for shape, dtype in results),
            in_specs=[away] * 4,
            out_specs=(whole,) * 4,
            scratch_shapes=[
                vmem((27, 4, 32), BF16),
                vmem((27, 32, 64), BF16),
                vmem((64, sy // 2, 64), BF16),
                vmem((64 * (sy // 2), LANES), F32),
                vmem((feats * rows, sx), BF16),
                vmem((feats * rows, sx), F32),
                vmem((2 * sz + 2, 2 * sy + 2, 16, sx), BF16),
                vmem((sz + 2, sy + 2, 32, sx), BF16),
                vmem((sz + 2, sy + 2, 64, sx), BF16),
                vmem((sz, sy, 256, sx), F32),
                vmem((sz, sy // 2, 256, 2 * sx), BF16),
                vmem((sy // 2, 64, sx), F32),
                vmem((8, 128, 256), BF16),
                vmem((256, 256), BF16),
                vmem((192, 288), BF16),
                vmem((96, 576), BF16),
                vmem((256, 256), F32),
                vmem((288, 256), F32),
                vmem((32 * rows, sx), F32),
                vmem((32 * rows, sx), F32),
                vmem((32 * rows, sx), BF16),
                vmem((32 * rows, sx), BF16),
                vmem((2, 16, 16, 128), F32),
                vmem((16, 16, 128), F32),
                vmem((16, 16, 128), F32),
                vmem((plane - 1, 16, 128), F32),
                vmem((16, 128), F32),
                vmem((nz, 16, 128), F32),
                vmem((2, 16, 16, 128), F32),
                vmem((1, 128, 128), F32),
                vmem((32, 128), F32),
                vmem((32, 128), F32),
                vmem((nz, 16, 128), F32),
                vmem((2, 16, 128), F32),
                vmem((plane, 16, 128), F32),
                vmem((2, 16, 128), F32),
                dma((6,)), dma((2,)), dma((2,)),
                dma((3, 6 + 2 * sz)), dma((3, 6 + 2 * sz)),
                pltpu.SemaphoreType.REGULAR((3,)), dma((4,)), dma((4,)),
                dma((2, nz - 1)), dma((2, nz - 1)),
                dma((3, plane - 1)), dma((3, plane - 1)),
            ],
            compiler_params=pltpu.CompilerParams(
                collective_id=0, has_side_effects=True, vmem_limit_bytes=48 * 2**20
            ),
        )(*(pltpu.with_memory_space_constraint(a, pltpu.HBM) for a in (vol, one, two, cot)))
        acts, grads, g_one, g_two = pl.pallas_call(
            leave_kernel,
            out_shape=tuple(jax.ShapeDtypeStruct(shape, dtype) for shape, dtype in results),
            in_specs=[whole] * 4,
            out_specs=(away,) * 4,
            scratch_shapes=[dma((4,))],
        )(*(pltpu.with_memory_space_constraint(a, pltpu.VMEM) for a in held))
        g_one = g_one.reshape(3, 3, 3, 4, 32).transpose(4, 3, 0, 1, 2)
        g_two = g_two.reshape(3, 3, 3, 32, 64).transpose(4, 3, 0, 1, 2)
        return acts.reshape(volumes.shape), grads.reshape(volumes.shape), g_one, g_two

    in_specs = (P("dp", None, "gz", "gy", None), P(), P(), P("dp", None, "gz", "gy", None))
    out_specs = (P("dp", None, "gz", "gy", None), P("dp", None, "gz", "gy", None), P(), P())
    return jax.shard_map(per_device, mesh=mesh, in_specs=in_specs, out_specs=out_specs, check_vma=False)
```

```python
import functools
import math

import jax
import jax.numpy as jnp
from jax import lax
from jax.experimental import pallas as pl
from jax.experimental.pallas import tpu as pltpu
from jax.sharding import PartitionSpec as P

LEAK = 0.3
REST = 1.0 - LEAK
LOG_TWO = math.log(2.0)
MESH = pl.DeviceIdType.MESH
F32 = jnp.float32
BF16 = jnp.bfloat16
LANES = 128
DIRS = tuple((dz, dy) for dz in (-1, 0, 1) for dy in (-1, 0, 1) if (dz, dy) != (0, 0))


def mm(a, b):
    return lax.dot_general(a, b, (((1,), (0,)), ((), ())), preferred_element_type=F32)


def mm_nt(a, b):
    return lax.dot_general(a, b, (((1,), (1,)), ((), ())), preferred_element_type=F32)


def eye(n, m):
    return (
        lax.broadcasted_iota(jnp.int32, (n, m), 0) == lax.broadcasted_iota(jnp.int32, (n, m), 1)
    ).astype(BF16)


def to_right(v):
    lane = lax.broadcasted_iota(jnp.int32, v.shape, 1)
    return jnp.where(lane == 0, 0.0, pltpu.roll(v, 1, axis=1))


def to_left(v):
    lane = lax.broadcasted_iota(jnp.int32, v.shape, 1)
    return jnp.where(lane == LANES - 1, 0.0, pltpu.roll(v, LANES - 1, axis=1))


def slope_of(v):
    return (LEAK + 0.5 * REST) + (0.5 * REST) * jnp.tanh(0.5 * v)


def part(d, n):
    if d == 0:
        return pl.ds(1, n), pl.ds(1, n)
    if d == 1:
        return pl.ds(n, 1), pl.ds(0, 1)
    return pl.ds(1, 1), pl.ds(n + 1, 1)


def step_kernel(
    dims,
    vol, one_in, two_in, cot_in,
    acts_out, grads_out, one_out, two_out,
    one_ref, two_ref, cot_ref, cotf, raw, rawf, fine, pool, grad2, slope1, shifted, cots, sel, w1, w2, wb,
    sum1, sum2, flat1, flat2, half1, half2,
    ga, rb, sc, rc, fd,
    qa, qs, qrb, qsc, qrc,
    local_sem, out_ssem, out_rsem,
    h_ssem, h_rsem,
    word_sem, line_ssem, line_rsem, plane_ssem, plane_rsem,
):
    nd, nz, ny, sz, sy, batch = dims
    rows = sz * sy
    core = lax.axis_index("pipe")
    iz, iy, idp = lax.axis_index("gz"), lax.axis_index("gy"), lax.axis_index("dp")
    other = 1 - core
    plane = nd * ny
    me_plane = idp * ny + iy

    def on_line(off):
        return lax.rem(iz + off, nz)

    def on_plane(off):
        q = lax.rem(me_plane + off, plane)
        return q, {"dp": q // ny, "gy": lax.rem(q, ny)}

    def exists(dz, dy):
        ok = jnp.bool_(True)
        if dz == 1:
            ok = jnp.logical_and(ok, iz < nz - 1)
        if dz == -1:
            ok = jnp.logical_and(ok, iz > 0)
        if dy == 1:
            ok = jnp.logical_and(ok, iy < ny - 1)
        if dy == -1:
            ok = jnp.logical_and(ok, iy > 0)
        return ok

    def neighbour(dz, dy):
        return {"gz": lax.rem(iz + dz + nz, nz), "gy": lax.rem(iy + dy + ny, ny)}

    def halo_copy(k, ref, d):
        dz, dy = DIRS[d]
        (fz, tz), (fy, ty) = part(dz, ref.shape[0] - 2), part(dy, ref.shape[1] - 2)
        return pltpu.make_async_remote_copy(
            src_ref=ref.at[fz, fy],
            dst_ref=ref.at[tz, ty],
            send_sem=h_ssem.at[k, d],
            recv_sem=h_rsem.at[k, d],
            device_id=neighbour(dz, dy),
            device_id_type=MESH,
        )

    turns = tuple(
        (p, dz, dy)
        for p in range(sz)
        for dz in (-1, 0, 1)
        for dy in (-1, 0, 1)
        if (dz, dy) != (0, 0) and (dz == 0 or p == (0 if dz == -1 else sz - 1))
    )

    def plane_copy(k, ref, m):
        p, dz, dy = turns[m]
        fy, ty = part(dy, ref.shape[1] - 2)
        to_z = p + 1 if dz == 0 else (0 if dz == 1 else sz + 1)
        return pltpu.make_async_remote_copy(
            src_ref=ref.at[p + 1, fy],
            dst_ref=ref.at[to_z, ty],
            send_sem=h_ssem.at[k, m],
            recv_sem=h_rsem.at[k, m],
            device_id=neighbour(dz, dy),
            device_id_type=MESH,
        )

    def plane_send(k, ref, p):
        for m, (q, dz, dy) in enumerate(turns):
            if q == p:

                @pl.when(exists(dz, dy))
                def _():
                    plane_copy(k, ref, m).start()

    def plane_arrive(k, ref, wanted):
        for m, (q, dz, dy) in enumerate(turns):
            if dz in wanted:

                @pl.when(exists(-dz, -dy))
                def _():
                    plane_copy(k, ref, m).wait_recv()

    def planes_sent(k, ref):
        for m, (q, dz, dy) in enumerate(turns):

            @pl.when(exists(dz, dy))
            def _():
                plane_copy(k, ref, m).wait_send()

    def halo_clear(ref):
        for dz, dy in DIRS:
            _, tz = part(dz, ref.shape[0] - 2)
            _, ty = part(dy, ref.shape[1] - 2)

            @pl.when(jnp.logical_not(exists(-dz, -dy)))
            def _():
                view = ref.at[tz, ty]
                view[...] = jnp.zeros(view.shape, view.dtype)

    def halo_send(k, ref):
        for d, (dz, dy) in enumerate(DIRS):

            @pl.when(exists(dz, dy))
            def _():
                halo_copy(k, ref, d).start()

    def halo_arrive(k, ref):
        for d, (dz, dy) in enumerate(DIRS):

            @pl.when(exists(-dz, -dy))
            def _():
                halo_copy(k, ref, d).wait_recv()

    def halo_sent(k, ref):
        for d, (dz, dy) in enumerate(DIRS):

            @pl.when(exists(dz, dy))
            def _():
                halo_copy(k, ref, d).wait_send()

    def to_line(k, off, src, dst, cross=False):
        there, at = {"gz": on_line(off)}, off - 1
        if cross:
            there, at = {**there, "pipe": other}, nz - 1 + off
        return pltpu.make_async_remote_copy(
            src_ref=src, dst_ref=dst, send_sem=line_ssem.at[k, at], recv_sem=line_rsem.at[k, at],
            device_id=there, device_id_type=MESH,
        )

    def to_plane(k, off, src, dst, cross=False):
        there, at = on_plane(off)[1], off - 1
        if cross:
            there, at = {**there, "pipe": other}, plane - 1 + off
        return pltpu.make_async_remote_copy(
            src_ref=src, dst_ref=dst, send_sem=plane_ssem.at[k, at], recv_sem=plane_rsem.at[k, at],
            device_id=there, device_id_type=MESH,
        )

    fetch = pltpu.make_async_copy(vol.at[core], raw, local_sem.at[0])
    fetch.start()
    fetch_more = [
        pltpu.make_async_copy(src, dst, local_sem.at[3 + k])
        for k, (src, dst) in enumerate(((one_in, one_ref), (two_in, two_ref), (cot_in.at[core], cot_ref)))
    ]
    for copy in fetch_more:
        copy.start()
    barrier = pltpu.get_barrier_semaphore()
    pl.semaphore_signal(barrier, inc=1, device_id={"pipe": other}, device_id_type=MESH)
    near = [
        {axis: lax.rem(at + step, size)}
        for axis, at, size in (("gz", iz, nz), ("gy", iy, ny), ("dp", idp, nd))
        for step in (1, size - 1)
    ]
    count = jnp.int32(1 + len(near))
    for there in near:
        pl.semaphore_signal(barrier, inc=1, device_id=there, device_id_type=MESH)
    for dz, dy in DIRS:
        if dz != 0 and dy != 0:

            @pl.when(exists(dz, dy))
            def _():
                pl.semaphore_signal(barrier, inc=1, device_id=neighbour(dz, dy), device_id_type=MESH)

            count = count + exists(dz, dy).astype(jnp.int32)

    def spread_word(r):
        for there in (*near, {"pipe": other}):
            pl.semaphore_signal(word_sem.at[r], inc=1, device_id=there, device_id_type=MESH)

    def hear_word(r):
        pl.semaphore_wait(word_sem.at[r], len(near) + 1)

    halo_clear(fine)
    halo_clear(pool)
    halo_clear(grad2)

    fetch.wait()
    rawf[...] = raw[...].astype(F32)

    def spread_row(z, y):
        t = rawf[pl.ds(z * sy + y, 32, stride=rows), :]
        sub = lax.broadcasted_iota(jnp.int32, t.shape, 0)
        odd = (sub & 4) != 0
        low = jnp.where(odd, to_right(t), t)
        high = jnp.where(odd, t, to_left(t))
        for a in range(2):
            for b in range(2):
                j = 8 * (2 * a + b)
                both = jnp.concatenate([low[j : j + 8], high[j : j + 8]], axis=0)
                fine[2 * z + a + 1, 2 * y + b + 1] = both.astype(BF16)

    def loop_rows(body):
        def outer(z, _):
            def inner(y, __):
                body(z, y)
                return 0

            lax.fori_loop(0, sy, inner, 0, unroll=4)
            return 0

        lax.fori_loop(0, sz, outer, 0)

    def loop_pairs(z, body, first=0, last=sy // 2):
        for p in range(first, last):
            body(z, p)

    up, down = tuple(range(sz)), tuple(reversed(range(sz)))

    def needs(order, z):
        wanted = () if z != order[0] else (0,)
        if z == 0:
            wanted += (1,)
        if z == sz - 1:
            wanted += (-1,)
        return wanted

    loop_rows(spread_row)
    pl.semaphore_wait(barrier, count)
    halo_send(0, fine)
    spread_word(0)

    for copy in fetch_more:
        copy.wait()
    row = lax.broadcasted_iota(jnp.int32, (128, 256), 0)
    lane = lax.broadcasted_iota(jnp.int32, (128, 256), 1)
    tap = row >> 2
    by3 = (tap * 11) >> 5
    by9 = (by3 * 11) >> 5
    tx, ty, tz = tap - 3 * by3, by3 - 3 * by9, by9
    for d in range(27):
        qa[0, 4 * d : 4 * d + 4, 0:32] = one_ref[d].astype(F32)
    qa[0, 108:128, 0:32] = jnp.zeros((20, 32), F32)
    one_t = mm_nt(eye(32, 32), qa[0, :, 0:32].astype(BF16)).astype(BF16)
    for s in range(8):
        a, b, c = s >> 2, (s >> 1) & 1, s & 1
        fx = tx + c
        slot = fx + 1 - 2 * (fx & 1)
        target = (tz + a) * 64 + (ty + b) * 16 + slot * 4 + (row & 3)
        hit = jnp.logical_and(lane == target, row < 108)
        sel[s] = jnp.where(hit, 1.0, 0.0).astype(BF16)
        w1[32 * s : 32 * s + 32, :] = mm(one_t, sel[s]).astype(BF16)
    for dx in range(3):
        taps = jnp.concatenate([two_ref[3 * j + dx] for j in range(9)], axis=0)
        w2[64 * dx : 64 * dx + 64, :] = mm_nt(eye(64, 64), taps).astype(BF16)
    for ex in range(3):
        blocks = [two_ref[3 * (8 - j) + 2 - ex].astype(F32) for j in range(9)]
        for j in range(0, 8, 2):
            pair = jnp.concatenate([blocks[j], blocks[j + 1]], axis=1)
            wb[32 * ex : 32 * ex + 32, 64 * j : 64 * j + 128] = pair.astype(BF16)
        wb[32 * ex : 32 * ex + 32, 512:576] = blocks[8].astype(BF16)
    double = (
        (lax.broadcasted_iota(jnp.int32, (64, LANES), 1) >> 1)
        == lax.broadcasted_iota(jnp.int32, (64, LANES), 0)
    ).astype(BF16)
    for o in range(64):
        cotf[4 * o : 4 * o + 4, 0:64] = cot_ref[o].astype(F32)
    for y in range(sy // 2):
        mine = cotf[pl.ds(y, 64, stride=sy // 2), :]
        cots[y] = mm(mine[:, 0:64].astype(BF16), double) * 0.125

    def windows(z, p):
        return jnp.concatenate(
            [fine[pl.ds(2 * z, 4), pl.ds(4 * p + 2 * j, 4)].reshape(256, LANES) for j in range(2)], axis=1
        )

    def first_pair(z, p):
        pre = mm(w1[...], windows(z, p))
        for j in range(2):
            y = 2 * p + j
            straight, product = None, None
            for s in range(8):
                v = pre[32 * s : 32 * s + 32, LANES * j : LANES * j + LANES]
                slope1[z, y, 32 * s : 32 * s + 32, :] = slope_of(v)
                bend, grown = jnp.maximum(v, LEAK * v), 1.0 + jnp.exp(-jnp.abs(v))
                straight = bend if s == 0 else straight + bend
                product = grown if s == 0 else product * grown
            mean = 0.125 * straight + (0.125 * REST) * jnp.log(product) - REST * LOG_TWO
            pool[z + 1, y + 1] = mean.astype(BF16)
            flat1[pl.ds(z * sy + y, 32, stride=rows), :] = mean

    hear_word(0)
    spread_word(1)
    halo_arrive(0, fine)
    hear_word(1)
    spread_word(2)
    for z in up:
        loop_pairs(z, first_pair)
        plane_send(1, pool, z)
    hear_word(2)
    spread_word(3)
    half1[...] = flat1[...].astype(BF16)

    def out_copies(k, half, out):
        here = pltpu.make_async_copy(half, out.at[core], local_sem.at[1 + k])
        there = pltpu.make_async_remote_copy(
            src_ref=half, dst_ref=out.at[core], send_sem=out_ssem.at[k], recv_sem=out_rsem.at[k],
            device_id={"pipe": other}, device_id_type=MESH,
        )
        return here, there

    for copy in out_copies(0, half1, acts_out):
        copy.start()

    def second_pair(z, p):
        cells = jnp.concatenate(
            [pool[pl.ds(z, 3), pl.ds(2 * p + j, 3)].reshape(288, LANES) for j in range(2)], axis=1
        )
        prod = mm(w2[...], cells)
        for j in range(2):
            mine = prod[:, LANES * j : LANES * j + LANES]
            pre = to_right(mine[0:64]) + mine[64:128] + to_left(mine[128:192])
            g = (slope_of(pre) * cots[p]).astype(BF16)
            grad2[z + 1, 2 * p + j + 1] = g
            wide = g.astype(F32)
            right = to_right(wide).astype(BF16)
            cols = slice(LANES * j, LANES * j + LANES)
            shifted[z, p, 0:64, cols] = to_left(wide).astype(BF16)
            shifted[z, p, 64:128, cols] = g
            shifted[z, p, 128:192, cols] = right
            shifted[z, p, 192:256, cols] = right

    for z in down:
        plane_arrive(1, pool, needs(down, z))
        loop_pairs(z, second_pair)
        plane_send(2, grad2, z)

    hear_word(3)

    pieces, sides = [], []
    for z in up:
        for y in range(sy):
            pieces.append(pool[pl.ds(z, 3), pl.ds(y, 3)].reshape(288, LANES))
        for p in range(sy // 2):
            sides.append(shifted[z, p])
    sum2[...] = mm_nt(jnp.concatenate(pieces, axis=1), jnp.concatenate(sides, axis=1))
    for r in range(18):
        ga[r // 16, r % 16] = sum2[16 * r : 16 * r + 16, 0:128].astype(BF16)
    keep = lax.broadcasted_iota(jnp.int32, (16, LANES), 1) < 64
    for r in range(9):
        lo, hi = sum2[16 * r : 16 * r + 16, 128:256], sum2[144 + 16 * r : 160 + 16 * r, 128:256]
        ga[1, 2 + r] = jnp.where(keep, lo, hi).astype(BF16)
    for r in range(11, 16):
        ga[1, r] = jnp.zeros((16, LANES), BF16)
    slot = core * plane + me_plane

    def scatter(off, cross=False):
        q = on_plane(off)[0]
        return to_plane(0, off, ga.at[other if cross else core, q], rb.at[slot], cross)

    rb[slot] = ga[core, me_plane]
    for off in range(plane):
        if off > 0:
            scatter(off).start()
        scatter(off, True).start()

    def back_pair(z, p):
        cells = jnp.concatenate(
            [grad2[pl.ds(z, 3), pl.ds(2 * p + j, 3)].reshape(576, LANES) for j in range(2)], axis=1
        )
        prod = mm(wb[...], cells)
        grads = []
        for j in range(2):
            y = 2 * p + j
            mine = prod[:, LANES * j : LANES * j + LANES]
            back = to_right(mine[0:32]) + mine[32:64] + to_left(mine[64:96])
            back = back.astype(BF16).astype(F32)
            flat2[pl.ds(z * sy + y, 32, stride=rows), :] = back
            eighth = back * 0.125
            grads.append(
                jnp.concatenate(
                    [(slope1[z, y, 32 * s : 32 * s + 32, :] * eighth).astype(BF16) for s in range(8)], axis=0
                )
            )
        return jnp.concatenate(grads, axis=1), windows(z, p)

    line = range(1, nz)
    flat = range(1, plane)

    for z in up:
        plane_arrive(2, grad2, needs(up, z))
        grads, cells = zip(*(back_pair(z, p) for p in range(sy // 2)))
        term = mm_nt(jnp.concatenate(grads, axis=1), jnp.concatenate(cells, axis=1))
        sum1[...] = term if z == up[0] else sum1[...] + term

    pieces = []
    for s in range(8):
        mine = sum1[32 * s : 32 * s + 32, :]
        high = mine.astype(BF16)
        low = (mine - high.astype(F32)).astype(BF16)
        pieces.append(jnp.concatenate([high, low], axis=0))
    folded = mm_nt(jnp.concatenate(pieces, axis=1), jnp.concatenate([sel[s] for s in range(8)], axis=1))
    folded = (folded[0:32] + folded[32:64]).astype(BF16)
    qs[0], qs[1] = folded[0:16], folded[16:32]
    qrc[slot] = qs[core]
    for off in range(plane):
        if off > 0:
            to_plane(1, off, qs.at[core], qrc.at[slot]).start()
        to_plane(1, off, qs.at[other], qrc.at[slot], True).start()

    for off in range(plane):
        if off > 0:
            scatter(off).wait_recv()
        scatter(off, True).wait_recv()
    total = rb[0].astype(F32)
    for q in range(1, 2 * plane):
        total = total + rb[q].astype(F32)
    total = total.astype(BF16)
    sc[...] = total
    rc[iz] = total
    for off in line:
        to_line(0, off, sc, rc.at[iz]).start()
    half2[...] = flat2[...].astype(BF16)
    for copy in out_copies(1, half2, grads_out):
        copy.start()

    for off in range(plane):
        if off > 0:
            to_plane(1, off, qs.at[core], qrc.at[slot]).wait_recv()
        to_plane(1, off, qs.at[other], qrc.at[slot], True).wait_recv()
    total = qrc[0].astype(F32)
    for q in range(1, 2 * plane):
        total = total + qrc[q].astype(F32)
    total = total.astype(BF16)
    qsc[...] = total
    qrb[core, iz] = total
    for off in range(nz):
        if off > 0:
            to_line(1, off, qsc, qrb.at[core, iz]).start()
        to_line(1, off, qsc, qrb.at[core, iz], True).start()

    for off in line:
        to_line(0, off, sc, rc.at[iz]).wait_recv()
    total = rc[0].astype(F32)
    for q in range(1, nz):
        total = total + rc[q].astype(F32)
    fd[core, me_plane] = (total * (1.0 / batch)).astype(BF16)
    for off in range(plane):
        if off > 0:
            to_plane(2, off, fd.at[core, me_plane], fd.at[core, me_plane]).start()
        to_plane(2, off, fd.at[core, me_plane], fd.at[core, me_plane], True).start()

    for off in range(nz):
        if off > 0:
            to_line(1, off, qsc, qrb.at[core, iz]).wait_recv()
        to_line(1, off, qsc, qrb.at[core, iz], True).wait_recv()
    halves = []
    for half in range(2):
        total = qrb[half, 0].astype(F32)
        for q in range(1, nz):
            total = total + qrb[half, q].astype(F32)
        halves.append(total * (1.0 / batch))
    turned = jnp.transpose(jnp.concatenate(halves, axis=0))
    for d in range(27):
        one_out[d] = turned[4 * d : 4 * d + 4, :]
    for off in range(plane):
        if off > 0:
            to_plane(2, off, fd.at[core, me_plane], fd.at[core, me_plane]).wait_recv()
        to_plane(2, off, fd.at[core, me_plane], fd.at[core, me_plane], True).wait_recv()
    for j in range(18):
        block = fd[j // 16, j % 16].astype(F32)
        rows16 = slice(16 * (j % 2), 16 * (j % 2) + 16)
        two_out[3 * (j // 2), rows16, :] = block[:, 0:64]
        two_out[3 * (j // 2) + 1, rows16, :] = pltpu.roll(block, 64, axis=1)[:, 0:64]
    for r in range(9):
        block = fd[1, 2 + r].astype(F32)
        for first, values in ((16 * r, block), (144 + 16 * r, pltpu.roll(block, 64, axis=1))):
            two_out[3 * (first // 32) + 2, first % 32 : first % 32 + 16, :] = values[:, 0:64]

    halo_sent(0, fine)
    planes_sent(1, pool)
    planes_sent(2, grad2)
    for off in line:
        to_line(0, off, sc, rc.at[iz]).wait_send()
        to_line(1, off, qsc, qrb.at[core, iz]).wait_send()
    for off in flat:
        scatter(off).wait_send()
        to_plane(1, off, qs.at[core], qrc.at[slot]).wait_send()
        to_plane(2, off, fd.at[core, me_plane], fd.at[core, me_plane]).wait_send()
    for off in range(nz):
        to_line(1, off, qsc, qrb.at[core, iz], True).wait_send()
    for off in range(plane):
        scatter(off, True).wait_send()
        to_plane(1, off, qs.at[other], qrc.at[slot], True).wait_send()
        to_plane(2, off, fd.at[core, me_plane], fd.at[core, me_plane], True).wait_send()
    for k, (half, out) in enumerate(((half1, acts_out), (half2, grads_out))):
        here, there = out_copies(k, half, out)
        here.wait()
        there.wait()


def leave_kernel(*refs):
    sem = refs[8]
    copies = [pltpu.make_async_copy(refs[k], refs[4 + k], sem.at[k]) for k in range(4)]
    for copy in copies:
        copy.start()
    for copy in copies:
        copy.wait()


def solution(mesh):
    nd, nz, ny = mesh.shape["dp"], mesh.shape["gz"], mesh.shape["gy"]
    plane = nd * ny

    def per_device(volumes, conv_one, conv_two, cotangent):
        micro, feats, sz, sy, sx = volumes.shape
        rows = sz * sy
        dims = (nd, nz, ny, sz, sy, micro * nd)
        vol = volumes.reshape(micro, feats * rows, sx)
        one = conv_one.transpose(2, 3, 4, 1, 0).reshape(27, 4, 32)
        two = conv_two.transpose(2, 3, 4, 1, 0).reshape(27, 32, 64)
        cot = cotangent[:, :, 0]
        whole = pl.BlockSpec(memory_space=pltpu.VMEM)
        away = pl.BlockSpec(memory_space=pltpu.HBM)
        vmem = pltpu.VMEM
        dma = pltpu.SemaphoreType.DMA
        results = ((vol.shape, BF16), (vol.shape, BF16), ((27, 4, 32), F32), ((27, 32, 64), F32))
        held = pl.pallas_call(
            functools.partial(step_kernel, dims),
            out_shape=tuple(vmem(shape, dtype) for shape, dtype in results),
            in_specs=[away] * 4,
            out_specs=(whole,) * 4,
            scratch_shapes=[
                vmem((27, 4, 32), BF16),
                vmem((27, 32, 64), BF16),
                vmem((64, sy // 2, 64), BF16),
                vmem((64 * (sy // 2), LANES), F32),
                vmem((feats * rows, sx), BF16),
                vmem((feats * rows, sx), F32),
                vmem((2 * sz + 2, 2 * sy + 2, 16, sx), BF16),
                vmem((sz + 2, sy + 2, 32, sx), BF16),
                vmem((sz + 2, sy + 2, 64, sx), BF16),
                vmem((sz, sy, 256, sx), F32),
                vmem((sz, sy // 2, 256, 2 * sx), BF16),
                vmem((sy // 2, 64, sx), F32),
                vmem((8, 128, 256), BF16),
                vmem((256, 256), BF16),
                vmem((192, 288), BF16),
                vmem((96, 576), BF16),
                vmem((256, 256), F32),
                vmem((288, 256), F32),
                vmem((32 * rows, sx), F32),
                vmem((32 * rows, sx), F32),
                vmem((32 * rows, sx), BF16),
                vmem((32 * rows, sx), BF16),
                vmem((2, plane, 16, 128), BF16),
                vmem((2 * plane, 16, 128), BF16),
                vmem((16, 128), BF16),
                vmem((nz, 16, 128), BF16),
                vmem((2, 16, 16, 128), BF16),
                vmem((1, 128, 128), F32),
                vmem((2, 16, 128), BF16),
                vmem((2, nz, 16, 128), BF16),
                vmem((16, 128), BF16),
                vmem((2 * plane, 16, 128), BF16),
                dma((6,)), dma((2,)), dma((2,)),
                dma((3, 6 + 2 * sz)), dma((3, 6 + 2 * sz)),
                pltpu.SemaphoreType.REGULAR((4,)),
                dma((2, 2 * nz - 1)), dma((2, 2 * nz - 1)),
                dma((3, 2 * plane - 1)), dma((3, 2 * plane - 1)),
            ],
            compiler_params=pltpu.CompilerParams(
                collective_id=0, has_side_effects=True, vmem_limit_bytes=48 * 2**20
            ),
        )(*(pltpu.with_memory_space_constraint(a, pltpu.HBM) for a in (vol, one, two, cot)))
        acts, grads, g_one, g_two = pl.pallas_call(
            leave_kernel,
            out_shape=tuple(jax.ShapeDtypeStruct(shape, dtype) for shape, dtype in results),
            in_specs=[whole] * 4,
            out_specs=(away,) * 4,
            scratch_shapes=[dma((4,))],
        )(*(pltpu.with_memory_space_constraint(a, pltpu.VMEM) for a in held))
        g_one = g_one.reshape(3, 3, 3, 4, 32).transpose(4, 3, 0, 1, 2)
        g_two = g_two.reshape(3, 3, 3, 32, 64).transpose(4, 3, 0, 1, 2)
        return acts.reshape(volumes.shape), grads.reshape(volumes.shape), g_one, g_two

    in_specs = (P("dp", None, "gz", "gy", None), P(), P(), P("dp", None, "gz", "gy", None))
    out_specs = (P("dp", None, "gz", "gy", None), P("dp", None, "gz", "gy", None), P(), P())
    return jax.shard_map(per_device, mesh=mesh, in_specs=in_specs, out_specs=out_specs, check_vma=False)
```

```python
import functools
import math

import jax
import jax.numpy as jnp
from jax import lax
from jax.experimental import pallas as pl
from jax.experimental.pallas import tpu as pltpu
from jax.sharding import PartitionSpec as P

LEAK = 0.3
REST = 1.0 - LEAK
LOG_TWO = math.log(2.0)
MESH = pl.DeviceIdType.MESH
F32 = jnp.float32
BF16 = jnp.bfloat16
LANES = 128
DIRS = ((-1, -1), (-1, 1), (1, -1), (1, 1), (0, -1), (0, 1), (-1, 0), (1, 0))


def mm(a, b):
    return lax.dot_general(a, b, (((1,), (0,)), ((), ())), preferred_element_type=F32)


def mm_nt(a, b):
    return lax.dot_general(a, b, (((1,), (1,)), ((), ())), preferred_element_type=F32)


def eye(n, m):
    return (
        lax.broadcasted_iota(jnp.int32, (n, m), 0) == lax.broadcasted_iota(jnp.int32, (n, m), 1)
    ).astype(BF16)


def to_right(v):
    lane = lax.broadcasted_iota(jnp.int32, v.shape, 1)
    return jnp.where(lane == 0, 0.0, pltpu.roll(v, 1, axis=1))


def to_left(v):
    lane = lax.broadcasted_iota(jnp.int32, v.shape, 1)
    return jnp.where(lane == LANES - 1, 0.0, pltpu.roll(v, LANES - 1, axis=1))


def slope_of(v):
    return (LEAK + 0.5 * REST) + (0.5 * REST) * jnp.tanh(0.5 * v)


def part(d, n):
    if d == 0:
        return pl.ds(1, n), pl.ds(1, n)
    if d == 1:
        return pl.ds(n, 1), pl.ds(0, 1)
    return pl.ds(1, 1), pl.ds(n + 1, 1)


def step_kernel(
    dims,
    vol, one_in, two_in, cot_in,
    acts_out, grads_out, one_out, two_out,
    one_ref, two_ref, cot_ref, cotf, raw, rawf, fine, pool, grad2, slope1, shifted, cots, sel, w1, w2, wb,
    sum1, sum2, flat1, flat2, half1, half2,
    ga, rb, sc, rc, fd,
    qa, qs, qrb, qsc, qrc,
    local_sem, out_ssem, out_rsem,
    h_ssem, h_rsem,
    word_sem, line_ssem, line_rsem, plane_ssem, plane_rsem,
):
    nd, nz, ny, sz, sy, batch = dims
    rows = sz * sy
    core = lax.axis_index("pipe")
    iz, iy, idp = lax.axis_index("gz"), lax.axis_index("gy"), lax.axis_index("dp")
    other = 1 - core
    plane = nd * ny
    me_plane = idp * ny + iy

    ring = lambda off, n: min(off % n, n - off % n)
    whole_line = sorted(range(nz), key=lambda off: -ring(off, nz))
    whole_plane = sorted(range(plane), key=lambda off: -ring(off, ny) - ring(off // ny, nd))
    line, flat = [off for off in whole_line if off], [off for off in whole_plane if off]

    def on_line(off):
        return lax.rem(iz + off, nz)

    def on_plane(off):
        q = lax.rem(me_plane + off, plane)
        return q, {"dp": q // ny, "gy": lax.rem(q, ny)}

    def exists(dz, dy):
        ok = jnp.bool_(True)
        if dz == 1:
            ok = jnp.logical_and(ok, iz < nz - 1)
        if dz == -1:
            ok = jnp.logical_and(ok, iz > 0)
        if dy == 1:
            ok = jnp.logical_and(ok, iy < ny - 1)
        if dy == -1:
            ok = jnp.logical_and(ok, iy > 0)
        return ok

    def neighbour(dz, dy):
        return {"gz": lax.rem(iz + dz + nz, nz), "gy": lax.rem(iy + dy + ny, ny)}

    def halo_copy(k, ref, d):
        dz, dy = DIRS[d]
        (fz, tz), (fy, ty) = part(dz, ref.shape[0] - 2), part(dy, ref.shape[1] - 2)
        return pltpu.make_async_remote_copy(
            src_ref=ref.at[fz, fy],
            dst_ref=ref.at[tz, ty],
            send_sem=h_ssem.at[k, d],
            recv_sem=h_rsem.at[k, d],
            device_id=neighbour(dz, dy),
            device_id_type=MESH,
        )

    turns = tuple(
        (p, dz, dy)
        for p in range(sz)
        for dz, dy in DIRS
        if dz == 0 or p == (0 if dz == -1 else sz - 1)
    )

    def plane_copy(k, ref, m):
        p, dz, dy = turns[m]
        fy, ty = part(dy, ref.shape[1] - 2)
        to_z = p + 1 if dz == 0 else (0 if dz == 1 else sz + 1)
        return pltpu.make_async_remote_copy(
            src_ref=ref.at[p + 1, fy],
            dst_ref=ref.at[to_z, ty],
            send_sem=h_ssem.at[k, m],
            recv_sem=h_rsem.at[k, m],
            device_id=neighbour(dz, dy),
            device_id_type=MESH,
        )

    def plane_send(k, ref, p):
        for m, (q, dz, dy) in enumerate(turns):
            if q == p:

                @pl.when(exists(dz, dy))
                def _():
                    plane_copy(k, ref, m).start()

    def plane_arrive(k, ref, wanted):
        for m, (q, dz, dy) in enumerate(turns):
            if dz in wanted:

                @pl.when(exists(-dz, -dy))
                def _():
                    plane_copy(k, ref, m).wait_recv()

    def planes_sent(k, ref):
        for m, (q, dz, dy) in enumerate(turns):

            @pl.when(exists(dz, dy))
            def _():
                plane_copy(k, ref, m).wait_send()

    def halo_clear(ref):
        for dz, dy in DIRS:
            _, tz = part(dz, ref.shape[0] - 2)
            _, ty = part(dy, ref.shape[1] - 2)

            @pl.when(jnp.logical_not(exists(-dz, -dy)))
            def _():
                view = ref.at[tz, ty]
                view[...] = jnp.zeros(view.shape, view.dtype)

    def halo_send(k, ref):
        for d, (dz, dy) in enumerate(DIRS):

            @pl.when(exists(dz, dy))
            def _():
                halo_copy(k, ref, d).start()

    def halo_arrive(k, ref):
        for d, (dz, dy) in enumerate(DIRS):

            @pl.when(exists(-dz, -dy))
            def _():
                halo_copy(k, ref, d).wait_recv()

    def halo_sent(k, ref):
        for d, (dz, dy) in enumerate(DIRS):

            @pl.when(exists(dz, dy))
            def _():
                halo_copy(k, ref, d).wait_send()

    def to_line(k, off, src, dst, cross=False):
        there, at = {"gz": on_line(off)}, off - 1
        if cross:
            there, at = {**there, "pipe": other}, nz - 1 + off
        return pltpu.make_async_remote_copy(
            src_ref=src, dst_ref=dst, send_sem=line_ssem.at[k, at], recv_sem=line_rsem.at[k, at],
            device_id=there, device_id_type=MESH,
        )

    def to_plane(k, off, src, dst, cross=False):
        there, at = on_plane(off)[1], off - 1
        if cross:
            there, at = {**there, "pipe": other}, plane - 1 + off
        return pltpu.make_async_remote_copy(
            src_ref=src, dst_ref=dst, send_sem=plane_ssem.at[k, at], recv_sem=plane_rsem.at[k, at],
            device_id=there, device_id_type=MESH,
        )

    fetch = pltpu.make_async_copy(vol.at[core], raw, local_sem.at[0])
    fetch.start()
    fetch_more = [
        pltpu.make_async_copy(src, dst, local_sem.at[3 + k])
        for k, (src, dst) in enumerate(((one_in, one_ref), (two_in, two_ref), (cot_in.at[core], cot_ref)))
    ]
    for copy in fetch_more:
        copy.start()
    barrier = pltpu.get_barrier_semaphore()
    pl.semaphore_signal(barrier, inc=1, device_id={"pipe": other}, device_id_type=MESH)
    near = [
        {axis: lax.rem(at + step, size)}
        for axis, at, size in (("gz", iz, nz), ("gy", iy, ny), ("dp", idp, nd))
        for step in (1, size - 1)
    ]
    count = jnp.int32(1 + len(near))
    for there in near:
        pl.semaphore_signal(barrier, inc=1, device_id=there, device_id_type=MESH)
    for dz, dy in DIRS:
        if dz != 0 and dy != 0:

            @pl.when(exists(dz, dy))
            def _():
                pl.semaphore_signal(barrier, inc=1, device_id=neighbour(dz, dy), device_id_type=MESH)

            count = count + exists(dz, dy).astype(jnp.int32)

    def spread_word(r):
        for there in (*near, {"pipe": other}):
            pl.semaphore_signal(word_sem.at[r], inc=1, device_id=there, device_id_type=MESH)

    def hear_word(r):
        pl.semaphore_wait(word_sem.at[r], len(near) + 1)

    halo_clear(fine)
    halo_clear(pool)
    halo_clear(grad2)

    fetch.wait()
    rawf[...] = raw[...].astype(F32)

    def spread_row(z, y):
        t = rawf[pl.ds(z * sy + y, 32, stride=rows), :]
        sub = lax.broadcasted_iota(jnp.int32, t.shape, 0)
        odd = (sub & 4) != 0
        low = jnp.where(odd, to_right(t), t)
        high = jnp.where(odd, t, to_left(t))
        for a in range(2):
            for b in range(2):
                j = 8 * (2 * a + b)
                both = jnp.concatenate([low[j : j + 8], high[j : j + 8]], axis=0)
                fine[2 * z + a + 1, 2 * y + b + 1] = both.astype(BF16)

    def loop_rows(body):
        def outer(z, _):
            def inner(y, __):
                body(z, y)
                return 0

            lax.fori_loop(0, sy, inner, 0, unroll=4)
            return 0

        lax.fori_loop(0, sz, outer, 0)

    def loop_pairs(z, body, first=0, last=sy // 2):
        for p in range(first, last):
            body(z, p)

    up, down = tuple(range(sz)), tuple(reversed(range(sz)))

    def needs(order, z):
        wanted = () if z != order[0] else (0,)
        if z == 0:
            wanted += (1,)
        if z == sz - 1:
            wanted += (-1,)
        return wanted

    loop_rows(spread_row)
    pl.semaphore_wait(barrier, count)
    halo_send(0, fine)
    spread_word(0)

    for copy in fetch_more:
        copy.wait()
    row = lax.broadcasted_iota(jnp.int32, (128, 256), 0)
    lane = lax.broadcasted_iota(jnp.int32, (128, 256), 1)
    tap = row >> 2
    by3 = (tap * 11) >> 5
    by9 = (by3 * 11) >> 5
    tx, ty, tz = tap - 3 * by3, by3 - 3 * by9, by9
    for d in range(27):
        qa[0, 4 * d : 4 * d + 4, 0:32] = one_ref[d].astype(F32)
    qa[0, 108:128, 0:32] = jnp.zeros((20, 32), F32)
    one_t = mm_nt(eye(32, 32), qa[0, :, 0:32].astype(BF16)).astype(BF16)
    for s in range(8):
        a, b, c = s >> 2, (s >> 1) & 1, s & 1
        fx = tx + c
        slot = fx + 1 - 2 * (fx & 1)
        target = (tz + a) * 64 + (ty + b) * 16 + slot * 4 + (row & 3)
        hit = jnp.logical_and(lane == target, row < 108)
        sel[s] = jnp.where(hit, 1.0, 0.0).astype(BF16)
        w1[32 * s : 32 * s + 32, :] = mm(one_t, sel[s]).astype(BF16)
    for dx in range(3):
        taps = jnp.concatenate([two_ref[3 * j + dx] for j in range(9)], axis=0)
        w2[64 * dx : 64 * dx + 64, :] = mm_nt(eye(64, 64), taps).astype(BF16)
    for ex in range(3):
        blocks = [two_ref[3 * (8 - j) + 2 - ex].astype(F32) for j in range(9)]
        for j in range(0, 8, 2):
            pair = jnp.concatenate([blocks[j], blocks[j + 1]], axis=1)
            wb[32 * ex : 32 * ex + 32, 64 * j : 64 * j + 128] = pair.astype(BF16)
        wb[32 * ex : 32 * ex + 32, 512:576] = blocks[8].astype(BF16)
    double = (
        (lax.broadcasted_iota(jnp.int32, (64, LANES), 1) >> 1)
        == lax.broadcasted_iota(jnp.int32, (64, LANES), 0)
    ).astype(BF16)
    for o in range(64):
        cotf[4 * o : 4 * o + 4, 0:64] = cot_ref[o].astype(F32)
    for y in range(sy // 2):
        mine = cotf[pl.ds(y, 64, stride=sy // 2), :]
        cots[y] = mm(mine[:, 0:64].astype(BF16), double) * 0.125

    def windows(z, p):
        return jnp.concatenate(
            [fine[pl.ds(2 * z, 4), pl.ds(4 * p + 2 * j, 4)].reshape(256, LANES) for j in range(2)], axis=1
        )

    def first_pair(z, p):
        pre = mm(w1[...], windows(z, p))
        for j in range(2):
            y = 2 * p + j
            straight, product = None, None
            for s in range(8):
                v = pre[32 * s : 32 * s + 32, LANES * j : LANES * j + LANES]
                slope1[z, y, 32 * s : 32 * s + 32, :] = v
                bend, grown = jnp.maximum(v, LEAK * v), 1.0 + jnp.exp(-jnp.abs(v))
                straight = bend if s == 0 else straight + bend
                product = grown if s == 0 else product * grown
            mean = 0.125 * straight + (0.125 * REST) * jnp.log(product) - REST * LOG_TWO
            pool[z + 1, y + 1] = mean.astype(BF16)
            flat1[pl.ds(z * sy + y, 32, stride=rows), :] = mean

    hear_word(0)
    spread_word(1)
    halo_arrive(0, fine)
    hear_word(1)
    spread_word(2)
    for z in up:
        loop_pairs(z, first_pair)
        plane_send(1, pool, z)
    hear_word(2)
    spread_word(3)
    half1[...] = flat1[...].astype(BF16)
    for z in range(sz):
        for y in range(sy):
            slope1[z, y] = slope_of(slope1[z, y])

    def out_copies(k, half, out):
        here = pltpu.make_async_copy(half, out.at[core], local_sem.at[1 + k])
        there = pltpu.make_async_remote_copy(
            src_ref=half, dst_ref=out.at[core], send_sem=out_ssem.at[k], recv_sem=out_rsem.at[k],
            device_id={"pipe": other}, device_id_type=MESH,
        )
        return here, there

    for copy in out_copies(0, half1, acts_out):
        copy.start()

    def second_pair(z, p):
        cells = jnp.concatenate(
            [pool[pl.ds(z, 3), pl.ds(2 * p + j, 3)].reshape(288, LANES) for j in range(2)], axis=1
        )
        prod = mm(w2[...], cells)
        for j in range(2):
            mine = prod[:, LANES * j : LANES * j + LANES]
            pre = to_right(mine[0:64]) + mine[64:128] + to_left(mine[128:192])
            grad2[z + 1, 2 * p + j + 1] = (slope_of(pre) * cots[p]).astype(BF16)

    def shift_pair(z, p):
        for j in range(2):
            g = grad2[z + 1, 2 * p + j + 1]
            wide = g.astype(F32)
            right = to_right(wide).astype(BF16)
            cols = slice(LANES * j, LANES * j + LANES)
            shifted[z, p, 0:64, cols] = to_left(wide).astype(BF16)
            shifted[z, p, 64:128, cols] = g
            shifted[z, p, 128:192, cols] = right
            shifted[z, p, 192:256, cols] = right

    for z in down:
        plane_arrive(1, pool, needs(down, z))
        loop_pairs(z, second_pair)
        plane_send(2, grad2, z)

    hear_word(3)

    pieces, sides = [], []
    for z in up:
        for y in range(sy):
            pieces.append(pool[pl.ds(z, 3), pl.ds(y, 3)].reshape(288, LANES))
        for p in range(sy // 2):
            shift_pair(z, p)
            sides.append(shifted[z, p])
    sum2[...] = mm_nt(jnp.concatenate(pieces, axis=1), jnp.concatenate(sides, axis=1))
    for r in range(18):
        ga[r // 16, r % 16] = sum2[16 * r : 16 * r + 16, 0:128].astype(BF16)
    keep = lax.broadcasted_iota(jnp.int32, (16, LANES), 1) < 64
    for r in range(9):
        lo, hi = sum2[16 * r : 16 * r + 16, 128:256], sum2[144 + 16 * r : 160 + 16 * r, 128:256]
        ga[1, 2 + r] = jnp.where(keep, lo, hi).astype(BF16)
    for r in range(11, 16):
        ga[1, r] = jnp.zeros((16, LANES), BF16)
    slot = core * plane + me_plane

    def scatter(off, cross=False):
        q = on_plane(off)[0]
        return to_plane(0, off, ga.at[other if cross else core, q], rb.at[slot], cross)

    rb[slot] = ga[core, me_plane]
    for off in whole_plane:
        if off > 0:
            scatter(off).start()
        scatter(off, True).start()

    def back_pair(z, p):
        cells = jnp.concatenate(
            [grad2[pl.ds(z, 3), pl.ds(2 * p + j, 3)].reshape(576, LANES) for j in range(2)], axis=1
        )
        prod = mm(wb[...], cells)
        grads = []
        for j in range(2):
            y = 2 * p + j
            mine = prod[:, LANES * j : LANES * j + LANES]
            back = to_right(mine[0:32]) + mine[32:64] + to_left(mine[64:96])
            back = back.astype(BF16).astype(F32)
            flat2[pl.ds(z * sy + y, 32, stride=rows), :] = back
            eighth = back * 0.125
            grads.append(
                jnp.concatenate(
                    [(slope1[z, y, 32 * s : 32 * s + 32, :] * eighth).astype(BF16) for s in range(8)], axis=0
                )
            )
        return jnp.concatenate(grads, axis=1), windows(z, p)


    for z in up:
        plane_arrive(2, grad2, needs(up, z))
        grads, cells = zip(*(back_pair(z, p) for p in range(sy // 2)))
        term = mm_nt(jnp.concatenate(grads, axis=1), jnp.concatenate(cells, axis=1))
        sum1[...] = term if z == up[0] else sum1[...] + term

    pieces = []
    for s in range(8):
        mine = sum1[32 * s : 32 * s + 32, :]
        high = mine.astype(BF16)
        low = (mine - high.astype(F32)).astype(BF16)
        pieces.append(jnp.concatenate([high, low], axis=0))
    folded = mm_nt(jnp.concatenate(pieces, axis=1), jnp.concatenate([sel[s] for s in range(8)], axis=1))
    folded = (folded[0:32] + folded[32:64]).astype(BF16)
    qs[0], qs[1] = folded[0:16], folded[16:32]
    qrc[slot] = qs[core]
    for off in whole_plane:
        if off > 0:
            to_plane(1, off, qs.at[core], qrc.at[slot]).start()
        to_plane(1, off, qs.at[other], qrc.at[slot], True).start()

    for off in whole_plane:
        if off > 0:
            scatter(off).wait_recv()
        scatter(off, True).wait_recv()
    total = rb[0].astype(F32)
    for q in range(1, 2 * plane):
        total = total + rb[q].astype(F32)
    total = total.astype(BF16)
    sc[...] = total
    rc[iz] = total
    for off in line:
        to_line(0, off, sc, rc.at[iz]).start()
    half2[...] = flat2[...].astype(BF16)
    for copy in out_copies(1, half2, grads_out):
        copy.start()

    for off in whole_plane:
        if off > 0:
            to_plane(1, off, qs.at[core], qrc.at[slot]).wait_recv()
        to_plane(1, off, qs.at[other], qrc.at[slot], True).wait_recv()
    total = qrc[0].astype(F32)
    for q in range(1, 2 * plane):
        total = total + qrc[q].astype(F32)
    total = total.astype(BF16)
    qsc[...] = total
    qrb[core, iz] = total
    for off in whole_line:
        if off > 0:
            to_line(1, off, qsc, qrb.at[core, iz]).start()
        to_line(1, off, qsc, qrb.at[core, iz], True).start()

    for off in line:
        to_line(0, off, sc, rc.at[iz]).wait_recv()
    total = rc[0].astype(F32)
    for q in range(1, nz):
        total = total + rc[q].astype(F32)
    fd[core, me_plane] = (total * (1.0 / batch)).astype(BF16)
    for off in whole_plane:
        if off > 0:
            to_plane(2, off, fd.at[core, me_plane], fd.at[core, me_plane]).start()
        to_plane(2, off, fd.at[core, me_plane], fd.at[core, me_plane], True).start()

    for off in whole_line:
        if off > 0:
            to_line(1, off, qsc, qrb.at[core, iz]).wait_recv()
        to_line(1, off, qsc, qrb.at[core, iz], True).wait_recv()
    halves = []
    for half in range(2):
        total = qrb[half, 0].astype(F32)
        for q in range(1, nz):
            total = total + qrb[half, q].astype(F32)
        halves.append(total * (1.0 / batch))
    turned = jnp.transpose(jnp.concatenate(halves, axis=0))
    for d in range(27):
        one_out[d] = turned[4 * d : 4 * d + 4, :]
    for off in whole_plane:
        if off > 0:
            to_plane(2, off, fd.at[core, me_plane], fd.at[core, me_plane]).wait_recv()
        to_plane(2, off, fd.at[core, me_plane], fd.at[core, me_plane], True).wait_recv()
    for j in range(18):
        block = fd[j // 16, j % 16].astype(F32)
        rows16 = slice(16 * (j % 2), 16 * (j % 2) + 16)
        two_out[3 * (j // 2), rows16, :] = block[:, 0:64]
        two_out[3 * (j // 2) + 1, rows16, :] = pltpu.roll(block, 64, axis=1)[:, 0:64]
    for r in range(9):
        block = fd[1, 2 + r].astype(F32)
        for first, values in ((16 * r, block), (144 + 16 * r, pltpu.roll(block, 64, axis=1))):
            two_out[3 * (first // 32) + 2, first % 32 : first % 32 + 16, :] = values[:, 0:64]

    halo_sent(0, fine)
    planes_sent(1, pool)
    planes_sent(2, grad2)
    for off in line:
        to_line(0, off, sc, rc.at[iz]).wait_send()
        to_line(1, off, qsc, qrb.at[core, iz]).wait_send()
    for off in flat:
        scatter(off).wait_send()
        to_plane(1, off, qs.at[core], qrc.at[slot]).wait_send()
        to_plane(2, off, fd.at[core, me_plane], fd.at[core, me_plane]).wait_send()
    for off in whole_line:
        to_line(1, off, qsc, qrb.at[core, iz], True).wait_send()
    for off in whole_plane:
        scatter(off, True).wait_send()
        to_plane(1, off, qs.at[other], qrc.at[slot], True).wait_send()
        to_plane(2, off, fd.at[core, me_plane], fd.at[core, me_plane], True).wait_send()
    for k, (half, out) in enumerate(((half1, acts_out), (half2, grads_out))):
        here, there = out_copies(k, half, out)
        here.wait()
        there.wait()


def leave_kernel(*refs):
    sem = refs[8]
    copies = [pltpu.make_async_copy(refs[k], refs[4 + k], sem.at[k]) for k in range(4)]
    for copy in copies:
        copy.start()
    for copy in copies:
        copy.wait()


def solution(mesh):
    nd, nz, ny = mesh.shape["dp"], mesh.shape["gz"], mesh.shape["gy"]
    plane = nd * ny

    def per_device(volumes, conv_one, conv_two, cotangent):
        micro, feats, sz, sy, sx = volumes.shape
        rows = sz * sy
        dims = (nd, nz, ny, sz, sy, micro * nd)
        vol = volumes.reshape(micro, feats * rows, sx)
        one = conv_one.transpose(2, 3, 4, 1, 0).reshape(27, 4, 32)
        two = conv_two.transpose(2, 3, 4, 1, 0).reshape(27, 32, 64)
        cot = cotangent[:, :, 0]
        whole = pl.BlockSpec(memory_space=pltpu.VMEM)
        away = pl.BlockSpec(memory_space=pltpu.HBM)
        vmem = pltpu.VMEM
        dma = pltpu.SemaphoreType.DMA
        results = ((vol.shape, BF16), (vol.shape, BF16), ((27, 4, 32), F32), ((27, 32, 64), F32))
        held = pl.pallas_call(
            functools.partial(step_kernel, dims),
            out_shape=tuple(vmem(shape, dtype) for shape, dtype in results),
            in_specs=[away] * 4,
            out_specs=(whole,) * 4,
            scratch_shapes=[
                vmem((27, 4, 32), BF16),
                vmem((27, 32, 64), BF16),
                vmem((64, sy // 2, 64), BF16),
                vmem((64 * (sy // 2), LANES), F32),
                vmem((feats * rows, sx), BF16),
                vmem((feats * rows, sx), F32),
                vmem((2 * sz + 2, 2 * sy + 2, 16, sx), BF16),
                vmem((sz + 2, sy + 2, 32, sx), BF16),
                vmem((sz + 2, sy + 2, 64, sx), BF16),
                vmem((sz, sy, 256, sx), F32),
                vmem((sz, sy // 2, 256, 2 * sx), BF16),
                vmem((sy // 2, 64, sx), F32),
                vmem((8, 128, 256), BF16),
                vmem((256, 256), BF16),
                vmem((192, 288), BF16),
                vmem((96, 576), BF16),
                vmem((256, 256), F32),
                vmem((288, 256), F32),
                vmem((32 * rows, sx), F32),
                vmem((32 * rows, sx), F32),
                vmem((32 * rows, sx), BF16),
                vmem((32 * rows, sx), BF16),
                vmem((2, plane, 16, 128), BF16),
                vmem((2 * plane, 16, 128), BF16),
                vmem((16, 128), BF16),
                vmem((nz, 16, 128), BF16),
                vmem((2, 16, 16, 128), BF16),
                vmem((1, 128, 128), F32),
                vmem((2, 16, 128), BF16),
                vmem((2, nz, 16, 128), BF16),
                vmem((16, 128), BF16),
                vmem((2 * plane, 16, 128), BF16),
                dma((6,)), dma((2,)), dma((2,)),
                dma((3, 6 + 2 * sz)), dma((3, 6 + 2 * sz)),
                pltpu.SemaphoreType.REGULAR((4,)),
                dma((2, 2 * nz - 1)), dma((2, 2 * nz - 1)),
                dma((3, 2 * plane - 1)), dma((3, 2 * plane - 1)),
            ],
            compiler_params=pltpu.CompilerParams(
                collective_id=0, has_side_effects=True, vmem_limit_bytes=48 * 2**20
            ),
        )(*(pltpu.with_memory_space_constraint(a, pltpu.HBM) for a in (vol, one, two, cot)))
        acts, grads, g_one, g_two = pl.pallas_call(
            leave_kernel,
            out_shape=tuple(jax.ShapeDtypeStruct(shape, dtype) for shape, dtype in results),
            in_specs=[whole] * 4,
            out_specs=(away,) * 4,
            scratch_shapes=[dma((4,))],
        )(*(pltpu.with_memory_space_constraint(a, pltpu.VMEM) for a in held))
        g_one = g_one.reshape(3, 3, 3, 4, 32).transpose(4, 3, 0, 1, 2)
        g_two = g_two.reshape(3, 3, 3, 32, 64).transpose(4, 3, 0, 1, 2)
        return acts.reshape(volumes.shape), grads.reshape(volumes.shape), g_one, g_two

    in_specs = (P("dp", None, "gz", "gy", None), P(), P(), P("dp", None, "gz", "gy", None))
    out_specs = (P("dp", None, "gz", "gy", None), P("dp", None, "gz", "gy", None), P(), P())
    return jax.shard_map(per_device, mesh=mesh, in_specs=in_specs, out_specs=out_specs, check_vma=False)
```

```python
import functools
import math

import jax
import jax.numpy as jnp
from jax import lax
from jax.experimental import pallas as pl
from jax.experimental.pallas import tpu as pltpu
from jax.sharding import PartitionSpec as P

LEAK = 0.3
REST = 1.0 - LEAK
LOG_TWO = math.log(2.0)
MESH = pl.DeviceIdType.MESH
F32 = jnp.float32
BF16 = jnp.bfloat16
LANES = 128
DIRS = ((-1, -1), (-1, 1), (1, -1), (1, 1), (0, -1), (0, 1), (-1, 0), (1, 0))


def mm(a, b):
    return lax.dot_general(a, b, (((1,), (0,)), ((), ())), preferred_element_type=F32)


def mm_nt(a, b):
    return lax.dot_general(a, b, (((1,), (1,)), ((), ())), preferred_element_type=F32)


def eye(n, m):
    return (
        lax.broadcasted_iota(jnp.int32, (n, m), 0) == lax.broadcasted_iota(jnp.int32, (n, m), 1)
    ).astype(BF16)


def to_right(v):
    lane = lax.broadcasted_iota(jnp.int32, v.shape, 1)
    return jnp.where(lane == 0, 0.0, pltpu.roll(v, 1, axis=1))


def to_left(v):
    lane = lax.broadcasted_iota(jnp.int32, v.shape, 1)
    return jnp.where(lane == LANES - 1, 0.0, pltpu.roll(v, LANES - 1, axis=1))


def slope_of(v):
    return (LEAK + 0.5 * REST) + (0.5 * REST) * jnp.tanh(0.5 * v)


def part(d, n):
    if d == 0:
        return pl.ds(1, n), pl.ds(1, n)
    if d == 1:
        return pl.ds(n, 1), pl.ds(0, 1)
    return pl.ds(1, 1), pl.ds(n + 1, 1)


def step_kernel(
    dims,
    vol, one_in, two_in, cot_in,
    acts_out, grads_out, one_out, two_out,
    one_ref, two_ref, cot_ref, cotf, raw, rawf, fine, pool, grad2, slope1, shifted, cots, sel, w1, w2, wb,
    sum1, sum2, flat1, flat2, half1, half2,
    ga, rb, sc, rc, fd,
    qa, qs, qrb, qsc, qrc,
    local_sem, out_ssem, out_rsem,
    h_ssem, h_rsem,
    word_sem, line_ssem, line_rsem, plane_ssem, plane_rsem,
):
    nd, nz, ny, sz, sy, batch = dims
    rows = sz * sy
    core = lax.axis_index("pipe")
    iz, iy, idp = lax.axis_index("gz"), lax.axis_index("gy"), lax.axis_index("dp")
    other = 1 - core
    plane = nd * ny
    me_plane = idp * ny + iy

    ring = lambda off, n: min(off % n, n - off % n)
    whole_line = sorted(range(nz), key=lambda off: -ring(off, nz))
    whole_plane = sorted(range(plane), key=lambda off: -ring(off, ny) - ring(off // ny, nd))
    line, flat = [off for off in whole_line if off], [off for off in whole_plane if off]

    def on_line(off):
        return lax.rem(iz + off, nz)

    def on_plane(off):
        q = lax.rem(me_plane + off, plane)
        return q, {"dp": q // ny, "gy": lax.rem(q, ny)}

    def exists(dz, dy):
        ok = jnp.bool_(True)
        if dz == 1:
            ok = jnp.logical_and(ok, iz < nz - 1)
        if dz == -1:
            ok = jnp.logical_and(ok, iz > 0)
        if dy == 1:
            ok = jnp.logical_and(ok, iy < ny - 1)
        if dy == -1:
            ok = jnp.logical_and(ok, iy > 0)
        return ok

    def neighbour(dz, dy):
        return {"gz": lax.rem(iz + dz + nz, nz), "gy": lax.rem(iy + dy + ny, ny)}

    def halo_copy(k, ref, d):
        dz, dy = DIRS[d]
        (fz, tz), (fy, ty) = part(dz, ref.shape[0] - 2), part(dy, ref.shape[1] - 2)
        return pltpu.make_async_remote_copy(
            src_ref=ref.at[fz, fy],
            dst_ref=ref.at[tz, ty],
            send_sem=h_ssem.at[k, d],
            recv_sem=h_rsem.at[k, d],
            device_id=neighbour(dz, dy),
            device_id_type=MESH,
        )

    turns = tuple(
        (p, dz, dy, h)
        for p in range(sz)
        for dz, dy in DIRS
        if dz == 0 or p == (0 if dz == -1 else sz - 1)
        for h in range(2)
        if dy == 0 or h == (0 if dy == -1 else 1)
    )

    def plane_copy(k, ref, m):
        p, dz, dy, h = turns[m]
        fy, ty = part(dy, sy) if dy else (pl.ds(1 + h * (sy // 2), sy // 2),) * 2
        to_z = p + 1 if dz == 0 else (0 if dz == 1 else sz + 1)
        return pltpu.make_async_remote_copy(
            src_ref=ref.at[p + 1, fy],
            dst_ref=ref.at[to_z, ty],
            send_sem=h_ssem.at[k, m],
            recv_sem=h_rsem.at[k, m],
            device_id=neighbour(dz, dy),
            device_id_type=MESH,
        )

    def plane_send(k, ref, p, half):
        for d in DIRS:
            group = [m for m, (q, dz, dy, h) in enumerate(turns) if q == p and (dz, dy) == d and h == half]
            if group:

                @pl.when(exists(*d))
                def _():
                    for m in group:
                        plane_copy(k, ref, m).start()

    def plane_arrive(k, ref, wanted):
        for d in DIRS:
            group = [m for m, (q, dz, dy, h) in enumerate(turns) if (dz, dy) == d and dz in wanted]
            if group:

                @pl.when(exists(-d[0], -d[1]))
                def _():
                    for m in group:
                        plane_copy(k, ref, m).wait_recv()

    def planes_sent(k, ref):
        for d in DIRS:
            group = [m for m, (q, dz, dy, h) in enumerate(turns) if (dz, dy) == d]

            @pl.when(exists(*d))
            def _():
                for m in group:
                    plane_copy(k, ref, m).wait_send()

    def halo_clear(ref):
        for dz, dy in DIRS:
            _, tz = part(dz, ref.shape[0] - 2)
            _, ty = part(dy, ref.shape[1] - 2)

            @pl.when(jnp.logical_not(exists(-dz, -dy)))
            def _():
                view = ref.at[tz, ty]
                view[...] = jnp.zeros(view.shape, view.dtype)

    def halo_send(k, ref):
        for d, (dz, dy) in enumerate(DIRS):

            @pl.when(exists(dz, dy))
            def _():
                halo_copy(k, ref, d).start()

    def halo_arrive(k, ref):
        for d, (dz, dy) in enumerate(DIRS):

            @pl.when(exists(-dz, -dy))
            def _():
                halo_copy(k, ref, d).wait_recv()

    def halo_sent(k, ref):
        for d, (dz, dy) in enumerate(DIRS):

            @pl.when(exists(dz, dy))
            def _():
                halo_copy(k, ref, d).wait_send()

    def to_line(k, off, src, dst, cross=False):
        there, at = {"gz": on_line(off)}, off - 1
        if cross:
            there, at = {**there, "pipe": other}, nz - 1 + off
        return pltpu.make_async_remote_copy(
            src_ref=src, dst_ref=dst, send_sem=line_ssem.at[k, at], recv_sem=line_rsem.at[k, at],
            device_id=there, device_id_type=MESH,
        )

    def to_plane(k, off, src, dst, cross=False):
        there, at = on_plane(off)[1], off - 1
        if cross:
            there, at = {**there, "pipe": other}, plane - 1 + off
        return pltpu.make_async_remote_copy(
            src_ref=src, dst_ref=dst, send_sem=plane_ssem.at[k, at], recv_sem=plane_rsem.at[k, at],
            device_id=there, device_id_type=MESH,
        )

    fetch = pltpu.make_async_copy(vol.at[core], raw, local_sem.at[0])
    fetch.start()
    fetch_more = [
        pltpu.make_async_copy(src, dst, local_sem.at[3 + k])
        for k, (src, dst) in enumerate(((one_in, one_ref), (two_in, two_ref), (cot_in.at[core], cot_ref)))
    ]
    for copy in fetch_more:
        copy.start()
    barrier = pltpu.get_barrier_semaphore()
    pl.semaphore_signal(barrier, inc=1, device_id={"pipe": other}, device_id_type=MESH)
    near = [
        {axis: lax.rem(at + step, size)}
        for axis, at, size in (("gz", iz, nz), ("gy", iy, ny), ("dp", idp, nd))
        for step in (1, size - 1)
    ]
    count = jnp.int32(1 + len(near))
    for there in near:
        pl.semaphore_signal(barrier, inc=1, device_id=there, device_id_type=MESH)
    for dz, dy in DIRS:
        if dz != 0 and dy != 0:

            @pl.when(exists(dz, dy))
            def _():
                pl.semaphore_signal(barrier, inc=1, device_id=neighbour(dz, dy), device_id_type=MESH)

            count = count + exists(dz, dy).astype(jnp.int32)

    def spread_word(r):
        for there in (*near, {"pipe": other}):
            pl.semaphore_signal(word_sem.at[r], inc=1, device_id=there, device_id_type=MESH)

    def hear_word(r):
        pl.semaphore_wait(word_sem.at[r], len(near) + 1)

    halo_clear(fine)
    halo_clear(pool)
    halo_clear(grad2)

    fetch.wait()
    rawf[...] = raw[...].astype(F32)

    def spread_row(z, y):
        t = rawf[pl.ds(z * sy + y, 32, stride=rows), :]
        sub = lax.broadcasted_iota(jnp.int32, t.shape, 0)
        odd = (sub & 4) != 0
        low = jnp.where(odd, to_right(t), t)
        high = jnp.where(odd, t, to_left(t))
        for a in range(2):
            for b in range(2):
                j = 8 * (2 * a + b)
                both = jnp.concatenate([low[j : j + 8], high[j : j + 8]], axis=0)
                fine[2 * z + a + 1, 2 * y + b + 1] = both.astype(BF16)

    def loop_rows(body):
        def outer(z, _):
            def inner(y, __):
                body(z, y)
                return 0

            lax.fori_loop(0, sy, inner, 0, unroll=4)
            return 0

        lax.fori_loop(0, sz, outer, 0)

    def loop_pairs(z, body, first=0, last=sy // 2):
        for p in range(first, last):
            body(z, p)

    up, down = tuple(range(sz)), tuple(reversed(range(sz)))

    def needs(order, z):
        wanted = () if z != order[0] else (0,)
        if z == 0:
            wanted += (1,)
        if z == sz - 1:
            wanted += (-1,)
        return wanted

    loop_rows(spread_row)
    pl.semaphore_wait(barrier, count)
    halo_send(0, fine)
    spread_word(0)

    for copy in fetch_more:
        copy.wait()
    row = lax.broadcasted_iota(jnp.int32, (128, 256), 0)
    lane = lax.broadcasted_iota(jnp.int32, (128, 256), 1)
    tap = row >> 2
    by3 = (tap * 11) >> 5
    by9 = (by3 * 11) >> 5
    tx, ty, tz = tap - 3 * by3, by3 - 3 * by9, by9
    for d in range(27):
        qa[0, 4 * d : 4 * d + 4, 0:32] = one_ref[d].astype(F32)
    qa[0, 108:128, 0:32] = jnp.zeros((20, 32), F32)
    one_t = mm_nt(eye(32, 32), qa[0, :, 0:32].astype(BF16)).astype(BF16)
    for s in range(8):
        a, b, c = s >> 2, (s >> 1) & 1, s & 1
        fx = tx + c
        slot = fx + 1 - 2 * (fx & 1)
        target = (tz + a) * 64 + (ty + b) * 16 + slot * 4 + (row & 3)
        hit = jnp.logical_and(lane == target, row < 108)
        sel[s] = jnp.where(hit, 1.0, 0.0).astype(BF16)
        w1[32 * s : 32 * s + 32, :] = mm(one_t, sel[s]).astype(BF16)
    for dx in range(3):
        taps = jnp.concatenate([two_ref[3 * j + dx] for j in range(9)], axis=0)
        w2[64 * dx : 64 * dx + 64, :] = mm_nt(eye(64, 64), taps).astype(BF16)
    for ex in range(3):
        blocks = [two_ref[3 * (8 - j) + 2 - ex].astype(F32) for j in range(9)]
        for j in range(0, 8, 2):
            pair = jnp.concatenate([blocks[j], blocks[j + 1]], axis=1)
            wb[32 * ex : 32 * ex + 32, 64 * j : 64 * j + 128] = pair.astype(BF16)
        wb[32 * ex : 32 * ex + 32, 512:576] = blocks[8].astype(BF16)
    double = (
        (lax.broadcasted_iota(jnp.int32, (64, LANES), 1) >> 1)
        == lax.broadcasted_iota(jnp.int32, (64, LANES), 0)
    ).astype(BF16)
    for o in range(64):
        cotf[4 * o : 4 * o + 4, 0:64] = cot_ref[o].astype(F32)
    for y in range(sy // 2):
        mine = cotf[pl.ds(y, 64, stride=sy // 2), :]
        cots[y] = mm(mine[:, 0:64].astype(BF16), double) * 0.125

    def windows(z, p):
        return jnp.concatenate(
            [fine[pl.ds(2 * z, 4), pl.ds(4 * p + 2 * j, 4)].reshape(256, LANES) for j in range(2)], axis=1
        )

    def first_pair(z, p):
        pre = mm(w1[...], windows(z, p))
        for j in range(2):
            y = 2 * p + j
            straight, product = None, None
            for s in range(8):
                v = pre[32 * s : 32 * s + 32, LANES * j : LANES * j + LANES]
                slope1[z, y, 32 * s : 32 * s + 32, :] = v
                bend, grown = jnp.maximum(v, LEAK * v), 1.0 + jnp.exp(-jnp.abs(v))
                straight = bend if s == 0 else straight + bend
                product = grown if s == 0 else product * grown
            mean = 0.125 * straight + (0.125 * REST) * jnp.log(product) - REST * LOG_TWO
            pool[z + 1, y + 1] = mean.astype(BF16)
            flat1[pl.ds(z * sy + y, 32, stride=rows), :] = mean

    hear_word(0)
    spread_word(1)
    halo_arrive(0, fine)
    hear_word(1)
    spread_word(2)
    for z in up:
        for h in range(2):
            loop_pairs(z, first_pair, h * (sy // 4), (h + 1) * (sy // 4))
            plane_send(1, pool, z, h)
    hear_word(2)
    spread_word(3)
    half1[...] = flat1[...].astype(BF16)
    for z in range(sz):
        for y in range(sy):
            slope1[z, y] = slope_of(slope1[z, y])

    def out_copies(k, half, out):
        here = pltpu.make_async_copy(half, out.at[core], local_sem.at[1 + k])
        there = pltpu.make_async_remote_copy(
            src_ref=half, dst_ref=out.at[core], send_sem=out_ssem.at[k], recv_sem=out_rsem.at[k],
            device_id={"pipe": other}, device_id_type=MESH,
        )
        return here, there

    for copy in out_copies(0, half1, acts_out):
        copy.start()

    def second_pair(z, p):
        cells = jnp.concatenate(
            [pool[pl.ds(z, 3), pl.ds(2 * p + j, 3)].reshape(288, LANES) for j in range(2)], axis=1
        )
        prod = mm(w2[...], cells)
        for j in range(2):
            mine = prod[:, LANES * j : LANES * j + LANES]
            pre = to_right(mine[0:64]) + mine[64:128] + to_left(mine[128:192])
            grad2[z + 1, 2 * p + j + 1] = (slope_of(pre) * cots[p]).astype(BF16)

    def shift_pair(z, p):
        for j in range(2):
            g = grad2[z + 1, 2 * p + j + 1]
            wide = g.astype(F32)
            right = to_right(wide).astype(BF16)
            cols = slice(LANES * j, LANES * j + LANES)
            shifted[z, p, 0:64, cols] = to_left(wide).astype(BF16)
            shifted[z, p, 64:128, cols] = g
            shifted[z, p, 128:192, cols] = right
            shifted[z, p, 192:256, cols] = right

    for z in down:
        plane_arrive(1, pool, needs(down, z))
        for h in range(2):
            loop_pairs(z, second_pair, h * (sy // 4), (h + 1) * (sy // 4))
            plane_send(2, grad2, z, h)

    hear_word(3)

    pieces, sides = [], []
    for z in up:
        for y in range(sy):
            pieces.append(pool[pl.ds(z, 3), pl.ds(y, 3)].reshape(288, LANES))
        for p in range(sy // 2):
            shift_pair(z, p)
            sides.append(shifted[z, p])
    sum2[...] = mm_nt(jnp.concatenate(pieces, axis=1), jnp.concatenate(sides, axis=1))
    for r in range(18):
        ga[r // 16, r % 16] = sum2[16 * r : 16 * r + 16, 0:128].astype(BF16)
    keep = lax.broadcasted_iota(jnp.int32, (16, LANES), 1) < 64
    for r in range(9):
        lo, hi = sum2[16 * r : 16 * r + 16, 128:256], sum2[144 + 16 * r : 160 + 16 * r, 128:256]
        ga[1, 2 + r] = jnp.where(keep, lo, hi).astype(BF16)
    for r in range(11, 16):
        ga[1, r] = jnp.zeros((16, LANES), BF16)
    slot = core * plane + me_plane

    def scatter(off, cross=False):
        q = on_plane(off)[0]
        return to_plane(0, off, ga.at[other if cross else core, q], rb.at[slot], cross)

    rb[slot] = ga[core, me_plane]
    for off in whole_plane:
        if off > 0:
            scatter(off).start()
        scatter(off, True).start()

    def back_pair(z, p):
        cells = jnp.concatenate(
            [grad2[pl.ds(z, 3), pl.ds(2 * p + j, 3)].reshape(576, LANES) for j in range(2)], axis=1
        )
        prod = mm(wb[...], cells)
        grads = []
        for j in range(2):
            y = 2 * p + j
            mine = prod[:, LANES * j : LANES * j + LANES]
            back = to_right(mine[0:32]) + mine[32:64] + to_left(mine[64:96])
            back = back.astype(BF16).astype(F32)
            flat2[pl.ds(z * sy + y, 32, stride=rows), :] = back
            eighth = back * 0.125
            grads.append(
                jnp.concatenate(
                    [(slope1[z, y, 32 * s : 32 * s + 32, :] * eighth).astype(BF16) for s in range(8)], axis=0
                )
            )
        return jnp.concatenate(grads, axis=1), windows(z, p)


    for z in up:
        plane_arrive(2, grad2, needs(up, z))
        grads, cells = zip(*(back_pair(z, p) for p in range(sy // 2)))
        term = mm_nt(jnp.concatenate(grads, axis=1), jnp.concatenate(cells, axis=1))
        sum1[...] = term if z == up[0] else sum1[...] + term

    pieces = []
    for s in range(8):
        mine = sum1[32 * s : 32 * s + 32, :]
        high = mine.astype(BF16)
        low = (mine - high.astype(F32)).astype(BF16)
        pieces.append(jnp.concatenate([high, low], axis=0))
    folded = mm_nt(jnp.concatenate(pieces, axis=1), jnp.concatenate([sel[s] for s in range(8)], axis=1))
    folded = (folded[0:32] + folded[32:64]).astype(BF16)
    qs[0], qs[1] = folded[0:16], folded[16:32]
    qrc[slot] = qs[core]
    for off in whole_plane:
        if off > 0:
            to_plane(1, off, qs.at[core], qrc.at[slot]).start()
        to_plane(1, off, qs.at[other], qrc.at[slot], True).start()

    for off in whole_plane:
        if off > 0:
            scatter(off).wait_recv()
        scatter(off, True).wait_recv()
    total = rb[0].astype(F32)
    for q in range(1, 2 * plane):
        total = total + rb[q].astype(F32)
    total = total.astype(BF16)
    sc[...] = total
    rc[iz] = total
    for off in line:
        to_line(0, off, sc, rc.at[iz]).start()
    half2[...] = flat2[...].astype(BF16)
    for copy in out_copies(1, half2, grads_out):
        copy.start()

    for off in whole_plane:
        if off > 0:
            to_plane(1, off, qs.at[core], qrc.at[slot]).wait_recv()
        to_plane(1, off, qs.at[other], qrc.at[slot], True).wait_recv()
    total = qrc[0].astype(F32)
    for q in range(1, 2 * plane):
        total = total + qrc[q].astype(F32)
    total = total.astype(BF16)
    qsc[...] = total
    qrb[core, iz] = total
    for off in whole_line:
        if off > 0:
            to_line(1, off, qsc, qrb.at[core, iz]).start()
        to_line(1, off, qsc, qrb.at[core, iz], True).start()

    for off in line:
        to_line(0, off, sc, rc.at[iz]).wait_recv()
    total = rc[0].astype(F32)
    for q in range(1, nz):
        total = total + rc[q].astype(F32)
    fd[core, me_plane] = (total * (1.0 / batch)).astype(BF16)
    for off in whole_plane:
        if off > 0:
            to_plane(2, off, fd.at[core, me_plane], fd.at[core, me_plane]).start()
        to_plane(2, off, fd.at[core, me_plane], fd.at[core, me_plane], True).start()

    for off in whole_line:
        if off > 0:
            to_line(1, off, qsc, qrb.at[core, iz]).wait_recv()
        to_line(1, off, qsc, qrb.at[core, iz], True).wait_recv()
    halves = []
    for half in range(2):
        total = qrb[half, 0].astype(F32)
        for q in range(1, nz):
            total = total + qrb[half, q].astype(F32)
        halves.append(total * (1.0 / batch))
    turned = jnp.transpose(jnp.concatenate(halves, axis=0))
    for d in range(27):
        one_out[d] = turned[4 * d : 4 * d + 4, :]
    for off in whole_plane:
        if off > 0:
            to_plane(2, off, fd.at[core, me_plane], fd.at[core, me_plane]).wait_recv()
        to_plane(2, off, fd.at[core, me_plane], fd.at[core, me_plane], True).wait_recv()
    for j in range(18):
        block = fd[j // 16, j % 16].astype(F32)
        rows16 = slice(16 * (j % 2), 16 * (j % 2) + 16)
        two_out[3 * (j // 2), rows16, :] = block[:, 0:64]
        two_out[3 * (j // 2) + 1, rows16, :] = pltpu.roll(block, 64, axis=1)[:, 0:64]
    for r in range(9):
        block = fd[1, 2 + r].astype(F32)
        for first, values in ((16 * r, block), (144 + 16 * r, pltpu.roll(block, 64, axis=1))):
            two_out[3 * (first // 32) + 2, first % 32 : first % 32 + 16, :] = values[:, 0:64]

    halo_sent(0, fine)
    planes_sent(1, pool)
    planes_sent(2, grad2)
    for off in line:
        to_line(0, off, sc, rc.at[iz]).wait_send()
        to_line(1, off, qsc, qrb.at[core, iz]).wait_send()
    for off in flat:
        scatter(off).wait_send()
        to_plane(1, off, qs.at[core], qrc.at[slot]).wait_send()
        to_plane(2, off, fd.at[core, me_plane], fd.at[core, me_plane]).wait_send()
    for off in whole_line:
        to_line(1, off, qsc, qrb.at[core, iz], True).wait_send()
    for off in whole_plane:
        scatter(off, True).wait_send()
        to_plane(1, off, qs.at[other], qrc.at[slot], True).wait_send()
        to_plane(2, off, fd.at[core, me_plane], fd.at[core, me_plane], True).wait_send()
    for k, (half, out) in enumerate(((half1, acts_out), (half2, grads_out))):
        here, there = out_copies(k, half, out)
        here.wait()
        there.wait()


def leave_kernel(*refs):
    sem = refs[8]
    copies = [pltpu.make_async_copy(refs[k], refs[4 + k], sem.at[k]) for k in range(4)]
    for copy in copies:
        copy.start()
    for copy in copies:
        copy.wait()


def solution(mesh):
    nd, nz, ny = mesh.shape["dp"], mesh.shape["gz"], mesh.shape["gy"]
    plane = nd * ny

    def per_device(volumes, conv_one, conv_two, cotangent):
        micro, feats, sz, sy, sx = volumes.shape
        rows = sz * sy
        dims = (nd, nz, ny, sz, sy, micro * nd)
        vol = volumes.reshape(micro, feats * rows, sx)
        one = conv_one.transpose(2, 3, 4, 1, 0).reshape(27, 4, 32)
        two = conv_two.transpose(2, 3, 4, 1, 0).reshape(27, 32, 64)
        cot = cotangent[:, :, 0]
        whole = pl.BlockSpec(memory_space=pltpu.VMEM)
        away = pl.BlockSpec(memory_space=pltpu.HBM)
        vmem = pltpu.VMEM
        dma = pltpu.SemaphoreType.DMA
        results = ((vol.shape, BF16), (vol.shape, BF16), ((27, 4, 32), F32), ((27, 32, 64), F32))
        held = pl.pallas_call(
            functools.partial(step_kernel, dims),
            out_shape=tuple(vmem(shape, dtype) for shape, dtype in results),
            in_specs=[away] * 4,
            out_specs=(whole,) * 4,
            scratch_shapes=[
                vmem((27, 4, 32), BF16),
                vmem((27, 32, 64), BF16),
                vmem((64, sy // 2, 64), BF16),
                vmem((64 * (sy // 2), LANES), F32),
                vmem((feats * rows, sx), BF16),
                vmem((feats * rows, sx), F32),
                vmem((2 * sz + 2, 2 * sy + 2, 16, sx), BF16),
                vmem((sz + 2, sy + 2, 32, sx), BF16),
                vmem((sz + 2, sy + 2, 64, sx), BF16),
                vmem((sz, sy, 256, sx), F32),
                vmem((sz, sy // 2, 256, 2 * sx), BF16),
                vmem((sy // 2, 64, sx), F32),
                vmem((8, 128, 256), BF16),
                vmem((256, 256), BF16),
                vmem((192, 288), BF16),
                vmem((96, 576), BF16),
                vmem((256, 256), F32),
                vmem((288, 256), F32),
                vmem((32 * rows, sx), F32),
                vmem((32 * rows, sx), F32),
                vmem((32 * rows, sx), BF16),
                vmem((32 * rows, sx), BF16),
                vmem((2, plane, 16, 128), BF16),
                vmem((2 * plane, 16, 128), BF16),
                vmem((16, 128), BF16),
                vmem((nz, 16, 128), BF16),
                vmem((2, 16, 16, 128), BF16),
                vmem((1, 128, 128), F32),
                vmem((2, 16, 128), BF16),
                vmem((2, nz, 16, 128), BF16),
                vmem((16, 128), BF16),
                vmem((2 * plane, 16, 128), BF16),
                dma((6,)), dma((2,)), dma((2,)),
                dma((3, 8 + 2 * sz)), dma((3, 8 + 2 * sz)),
                pltpu.SemaphoreType.REGULAR((4,)),
                dma((2, 2 * nz - 1)), dma((2, 2 * nz - 1)),
                dma((3, 2 * plane - 1)), dma((3, 2 * plane - 1)),
            ],
            compiler_params=pltpu.CompilerParams(
                collective_id=0, has_side_effects=True, vmem_limit_bytes=48 * 2**20
            ),
        )(*(pltpu.with_memory_space_constraint(a, pltpu.HBM) for a in (vol, one, two, cot)))
        acts, grads, g_one, g_two = pl.pallas_call(
            leave_kernel,
            out_shape=tuple(jax.ShapeDtypeStruct(shape, dtype) for shape, dtype in results),
            in_specs=[whole] * 4,
            out_specs=(away,) * 4,
            scratch_shapes=[dma((4,))],
        )(*(pltpu.with_memory_space_constraint(a, pltpu.VMEM) for a in held))
        g_one = g_one.reshape(3, 3, 3, 4, 32).transpose(4, 3, 0, 1, 2)
        g_two = g_two.reshape(3, 3, 3, 32, 64).transpose(4, 3, 0, 1, 2)
        return acts.reshape(volumes.shape), grads.reshape(volumes.shape), g_one, g_two

    in_specs = (P("dp", None, "gz", "gy", None), P(), P(), P("dp", None, "gz", "gy", None))
    out_specs = (P("dp", None, "gz", "gy", None), P("dp", None, "gz", "gy", None), P(), P())
    return jax.shard_map(per_device, mesh=mesh, in_specs=in_specs, out_specs=out_specs, check_vma=False)
```
